32 devices in a mesh: ep: 8 (over y, x, core), dp: 4 (over z).
Axes of the slice: x: 2, y: 2, z: 4, core: 2. Of those that a mesh axis runs over, the one named last changes fastest.
Arguments:
- out_grad: bfloat16 [4, 1024, 2048], P('dp', 'ep'), may hold values from -6 to 6
- gates: bfloat16 [4, 1024, 8], P('dp', 'ep'), may hold values from 0.019897461 to 0.5
- routes: int32 [4, 1024, 8], P('dp', 'ep'), may hold values from 0 to 31, all different within a row; in each aligned block of 128 rows (0 to 127, 128 to 255, ..., all dimensions but the last counted through in order) at most 48 rows name the same one
- expert_slot: int32 [32], replicated, may hold values from 0 to 31, each once
- hidden_saved: bfloat16 [4, 32, 8, 48, 768], P('dp', 'ep'), may hold values from -6 to 6
- w_down: bfloat16 [2048, 24576], P('dp', 'ep'), may hold values from -0.21875 to 0.21875
Outputs:
- hidden_grad: bfloat16 [4, 32, 8, 48, 768], P('dp', 'ep')
- gate_grad: float32 [4, 1024, 8], P('dp', 'ep')
- weight_grad: float32 [2048, 24576], P('dp', 'ep')
The draws below stay inside these ranges and needn't reach their ends.
Inputs may be any that keep to these rules, and one draw needn't show every extreme that they name: `routes`: the rows of one device name no expert more than 48 times, and every expert is named by some row. `expert_slot`: each slot once.
All inputs are finite; a program needn't handle non-finite values.
Results may differ from the reference program's by a relative error of at most 0.012.
Values may be sent and summed in bfloat16 or wider, within the bound.
No kernel may reach another device: no remote copies, remote signals or barrier semaphores. Data moves between devices by JAX's collectives and lax.ppermute only.
A program may use at most 128 MiB of HBM per device.

```python
import math
import jax
import jax.numpy as jnp
import numpy as np
from jax import lax

D = 2048
H = 768
TOPK = 8
TOK_DEV = 128
EXPERTS = 32
CAP = 48
GROUP_TOK = 1024
N_EP = 8
N_DP = 4


def block_scale(rng, shape, split, smallest, largest):
    loudness = 1.0
    for position, parts in split:
        steps = jax.random.uniform(jax.random.fold_in(jax.random.fold_in(rng, 6), position), (parts,), jnp.float32, smallest / len(split), largest / len(split))
        loudness = loudness * jnp.repeat(jnp.exp(steps), shape[position] // parts).reshape((-1,) + (1,) * (len(shape) - 1 - position))
    return loudness


def routed_block(stream_key, own, number, rows, count, top, reach, lean):
    ranking = jax.random.permutation(stream_key, count)
    heavy_load, common = load_shares(count, rows * top, reach, lean, True), load_shares(count, rows * top, reach, lean, False)
    places = jnp.arange(count)

    def named(lengths, rotation):
        used = int((lengths > 0).sum())
        fixed = max(1, used // 4)
        passed = fixed + (places - fixed + rotation * (used - fixed)) % max(1, count - fixed)
        return jnp.zeros((count,), jnp.int32).at[ranking[jnp.where(places < fixed, places, passed)]].set(jnp.asarray(lengths, jnp.int32))

    lengths = jnp.where(number % 4 == 0, named(heavy_load, number // 4), named(common, number - number // 4 - 1))
    mixed = jax.random.permutation(jax.random.fold_in(own, 3), count)
    source_of, taker = mixed[0:count // 2 * 2:2], mixed[1:count // 2 * 2:2]
    slack = jnp.minimum(lengths[source_of] - 1, reach - lengths[taker]) // 2
    slack = jnp.where((source_of == ranking[0]) | (taker == ranking[0]) | (lengths[taker] == 0), 0, jnp.maximum(slack, 0))
    passed = jax.random.randint(jax.random.fold_in(own, 4), (count // 2,), 0, 1 << 20) % (slack + 1)
    lengths = lengths.at[source_of].add(-passed).at[taker].add(passed)
    members = jnp.searchsorted(jnp.cumsum(lengths), jnp.arange(rows * top), side="right").astype(jnp.int32)
    listing = members.reshape(top, rows).T
    listing = listing[jax.random.permutation(jax.random.fold_in(own, 1), rows)]
    rotation = jax.random.randint(jax.random.fold_in(own, 2), (rows, 1), 0, top)
    return jnp.take_along_axis(listing, (jnp.arange(top)[None, :] + rotation) % top, axis=1)


def load_shares(number_of, total, most, slope, full):
    loads = [(1 << 20) // math.isqrt(standing ** slope) + 1 for standing in range(1, number_of + 1)]
    largest = most if full else min(most, max(-(-total // number_of), total * loads[0] // sum(loads)))
    least = 1 if total - largest >= number_of - 1 else 0
    counts, spare = [largest] + [least] * (number_of - 1), total - largest - least * (number_of - 1)
    while spare > 0:
        candidates = [i for i in range(1, number_of) if counts[i] < largest] or [i for i in range(1, number_of) if counts[i] < most]
        whole, budget = sum([loads[i] for i in candidates]), spare
        for i in candidates:
            extra = min(most - counts[i], max(1, budget * loads[i] // whole), spare)
            counts[i] = counts[i] + extra
            spare = spare - extra
    return np.array(counts)


def centred(rng, shape, spread, bound, pieces=(), kind=jnp.bfloat16):
    drawn = jax.random.normal(rng, shape, jnp.float32) * spread
    if len(pieces) > 0:
        drawn = block_scale(rng, shape, pieces, -0.22, 0.18) * drawn
    return jnp.clip(drawn, min=-bound, max=bound).astype(kind)


def setup_inputs(seed: int = 0) -> dict:
    splits = jax.random.split(jax.random.key(seed), 7)
    out_grad = centred(splits[0], (N_DP, GROUP_TOK, D), 1.0, 6.0, ((0, 4), (1, 8)))
    gates = jnp.clip(0.019897461 + 0.48010254 * jax.random.uniform(splits[1], (N_DP, GROUP_TOK, TOPK), jnp.float32) ** block_scale(splits[1], (N_DP, GROUP_TOK, TOPK), ((0, 4), (1, 8)), -0.2, 0.2), 0.019897461, 0.5).astype(jnp.bfloat16)
    routes_keys = jax.random.split(jax.random.fold_in(splits[2], 1), N_DP * GROUP_TOK // TOK_DEV)
    routes_turns = jax.random.permutation(jax.random.fold_in(splits[2], 3), N_DP * GROUP_TOK // TOK_DEV)
    routes = jax.vmap(lambda own, number: routed_block(jax.random.fold_in(splits[2], 2), own, number, TOK_DEV, EXPERTS, TOPK, CAP, 2))(routes_keys, routes_turns).reshape((N_DP, GROUP_TOK, TOPK))
    expert_slot = jax.random.permutation(splits[3], EXPERTS).astype(jnp.int32)
    hidden_saved = centred(splits[4], (N_DP, EXPERTS, N_EP, CAP, H), 1.0, 6.0, ((0, 4), (1, 8)))
    w_down = centred(splits[5], (D, EXPERTS * H), H ** -0.5, 0.21875, ((0, 4), (1, 8)))
    return {"out_grad": out_grad, "gates": gates, "routes": routes, "expert_slot": expert_slot, "hidden_saved": hidden_saved, "w_down": w_down}


def group_pass(weight_sum, items, expert_slot, w_full):
    out_rows, gate_rows, route_rows, saved = items
    flat_ids = route_rows.reshape(N_EP, TOK_DEV * TOPK)
    onehot = (flat_ids[:, :, None] == jnp.arange(EXPERTS, dtype=jnp.int32)[None, None, :]).astype(jnp.int32)
    slot_ids = jnp.sum(onehot * expert_slot[None, None, :], axis=2).astype(jnp.int32)
    ranks = jnp.sum(onehot * (jnp.cumsum(onehot, axis=1) - 1), axis=2).astype(jnp.int32)
    target = (slot_ids * CAP + ranks).astype(jnp.int32)
    sources = jnp.broadcast_to(jnp.arange(N_EP, dtype=jnp.int32)[:, None], target.shape)
    rows = jnp.repeat(out_rows.reshape(N_EP, TOK_DEV, D), TOPK, axis=1)
    gate_vals = gate_rows.reshape(N_EP, TOK_DEV * TOPK)
    sent = jnp.zeros((N_EP, EXPERTS * CAP, D), jnp.bfloat16).at[sources, target].set(rows)
    sent_gates = jnp.zeros((N_EP, EXPERTS * CAP), jnp.bfloat16).at[sources, target].set(gate_vals)
    sent = sent.reshape(N_EP, EXPERTS, CAP, D)
    gates_qsc = sent_gates.reshape(N_EP, EXPERTS, CAP).transpose(1, 0, 2).astype(jnp.float32)
    u = jnp.einsum('sqcd,dqj->qscj', sent.astype(jnp.float32), w_full.astype(jnp.float32))
    hidden_grad = (gates_qsc[..., None] * u).astype(jnp.bfloat16)
    slot_grad = jnp.sum(saved.astype(jnp.float32) * u, axis=3)
    by_source = slot_grad.transpose(1, 0, 2).reshape(N_EP, EXPERTS * CAP)
    gate_grad = jnp.take_along_axis(by_source, target, axis=1).reshape(N_EP * TOK_DEV, TOPK)
    scaled = (gates_qsc[..., None] * saved.astype(jnp.float32)).astype(jnp.bfloat16)
    partial_value = jnp.einsum('sqcd,qscj->dqj', sent.astype(jnp.float32), scaled.astype(jnp.float32)).astype(jnp.bfloat16)
    weight_sum = weight_sum + partial_value.reshape(D, EXPERTS * H).astype(jnp.float32)
    return weight_sum, (hidden_grad, gate_grad)


def reference(out_grad, gates, routes, expert_slot, hidden_saved, w_down):
    w_full = w_down.reshape(D, EXPERTS, H)
    start = jnp.zeros((D, EXPERTS * H), jnp.float32)

    def step(carry, items):
        return group_pass(carry, items, expert_slot, w_full)

    weight_grad, (hidden_grad, gate_grad) = lax.scan(step, start, (out_grad, gates, routes, hidden_saved))
    return hidden_grad, gate_grad, weight_grad
```

```python
import functools

import jax
import jax.numpy as jnp
from jax import lax
from jax.experimental import pallas as pl
from jax.experimental.pallas import tpu as pltpu
from jax.sharding import PartitionSpec as P


BF = jnp.bfloat16
F32 = jnp.float32
CHUNKS = 2


def cost(flops, nbytes):
    return pl.CostEstimate(flops=int(flops), bytes_accessed=int(nbytes), transcendentals=0)


def dot(a, b):
    return jnp.dot(a, b, preferred_element_type=F32)


def pack_kernel(x_ref, r_ref, g_ref, o_ref, turn):
    tokens, chosen = r_ref.shape

    @pl.when(pl.program_id(0) == 0)
    def _():
        turn[...] = jnp.zeros_like(turn)
        turn[:, :chosen] = r_ref[...].astype(F32)
        turn[:, chosen : 2 * chosen] = g_ref[...].astype(F32)

    o_ref[0, :tokens, :] = x_ref[...]
    o_ref[0, tokens:, :] = jnp.zeros((o_ref.shape[1] - tokens, o_ref.shape[2]), BF)
    o_ref[0, tokens : tokens + 2 * chosen, :tokens] = turn[...].T[: 2 * chosen].astype(BF)


def pack(x, routes, gates, n):
    tokens, width = x.shape
    chosen = routes.shape[1]
    part = width // n
    extra = -(-2 * chosen // 16) * 16
    return pl.pallas_call(
        pack_kernel,
        grid=(n,),
        in_specs=[
            pl.BlockSpec((tokens, part), lambda k: (0, k)),
            pl.BlockSpec((tokens, chosen), lambda k: (0, 0)),
            pl.BlockSpec((tokens, chosen), lambda k: (0, 0)),
        ],
        out_specs=pl.BlockSpec((1, tokens + extra, part), lambda k: (k, 0, 0)),
        out_shape=jax.ShapeDtypeStruct((n, tokens + extra, part), BF),
        scratch_shapes=[pltpu.VMEM((tokens, tokens), F32)],
        cost_estimate=cost(0, 4 * tokens * width),
        name="pack",
    )(x, routes, gates)


def dispatch_kernel(dims, sc, *refs):
    sources, local_experts, slots, tokens, chosen = dims
    pieces, (rows_ref, tgt_ref), (hit, gate) = refs[:sources], refs[sources:-2], refs[-2:]
    pad = tgt_ref.shape[2]
    me = sc[1]
    line = lax.broadcasted_iota(jnp.int32, (pad, tokens), 0)
    for m in range(sources):
        info = pieces[m][0, tokens : tokens + 2 * chosen, :tokens].astype(F32)
        named, weights = info[:chosen], info[chosen:]
        hits = jnp.zeros((pad, tokens), F32)
        vals = jnp.zeros((pad, tokens), F32)
        for l in range(local_experts):
            same = named == sc[2 + me * local_experts + l].astype(F32)
            one = jnp.sum(jnp.where(same, 1.0, 0.0), axis=0, keepdims=True)
            val = jnp.sum(jnp.where(same, weights, 0.0), axis=0, keepdims=True)
            hits = jnp.where(line == l, one, hits)
            vals = jnp.where(line == l, val, vals)
        hit[m * pad : (m + 1) * pad] = hits
        gate[m * pad : (m + 1) * pad] = vals
    earlier = lax.broadcasted_iota(jnp.int32, (tokens, tokens), 0) < lax.broadcasted_iota(
        jnp.int32, (tokens, tokens), 1
    )
    rank = dot(hit[...].astype(BF), jnp.where(earlier, 1.0, 0.0).astype(BF))
    for m in range(sources):
        first = ((me ^ m) * slots).astype(F32)
        block = slice(m * pad, (m + 1) * pad)
        tgt_ref[0, m] = jnp.where(hit[block] > 0.5, rank[block] + first, -1.0)
    if slots % 16 == 0:
        place = lax.broadcasted_iota(jnp.int32, (slots, tokens), 0).astype(F32)
        for m in range(sources):
            s = me ^ m
            here = place + (s * slots).astype(F32)
            pick = [
                jnp.where(
                    here == tgt_ref[0, m, l : l + 1, :],
                    gate[m * pad + l : m * pad + l + 1, :],
                    0.0,
                ).astype(BF)
                for l in range(local_experts)
            ]
            got = dot(jnp.concatenate(pick, axis=0), pieces[m][0, :tokens, :]).astype(BF)
            for l in range(local_experts):
                rows_ref[0, l, pl.ds(pl.multiple_of(s * slots, 16), slots), :] = got[
                    l * slots : (l + 1) * slots
                ]
    else:
        here = lax.broadcasted_iota(jnp.int32, (sources * slots, tokens), 0).astype(F32)
        for l in range(local_experts):
            total = jnp.zeros((sources * slots, rows_ref.shape[3]), F32)
            for m in range(sources):
                pick = jnp.where(
                    here == tgt_ref[0, m, l : l + 1, :],
                    gate[m * pad + l : m * pad + l + 1, :],
                    0.0,
                ).astype(BF)
                total += dot(pick, pieces[m][0, :tokens, :])
            rows_ref[0, l] = total.astype(BF)


def dispatch(sc, pieces, local_experts, slots, tokens, chosen):
    sources = len(pieces)
    n, height, part = pieces[0].shape
    pad = -(-local_experts // 8) * 8
    depth = sources * slots
    return pl.pallas_call(
        functools.partial(dispatch_kernel, (sources, local_experts, slots, tokens, chosen)),
        grid_spec=pltpu.PrefetchScalarGridSpec(
            num_scalar_prefetch=1,
            grid=(n,),
            in_specs=[pl.BlockSpec((1, height, part), lambda g, sc: (g, 0, 0))] * sources,
            out_specs=[
                pl.BlockSpec((1, local_experts, depth, part), lambda g, sc: (g, 0, 0, 0)),
                pl.BlockSpec((1, sources, pad, tokens), lambda g, sc: (g, 0, 0, 0)),
            ],
            scratch_shapes=[pltpu.VMEM((sources * pad, tokens), F32)] * 2,
        ),
        out_shape=[
            jax.ShapeDtypeStruct((n, local_experts, depth, part), BF),
            jax.ShapeDtypeStruct((n, sources, pad, tokens), F32),
        ],
        cost_estimate=cost(
            2 * n * sources * local_experts * slots * tokens * part,
            2 * n * part * (sources * height + local_experts * depth),
        ),
        name="dispatch",
    )(sc, *pieces)


def turn_group(n, t, way, z):
    return jnp.clip(n + 1 - t + z if way > 0 else t - n - 1 + z, 0, n - 1)


def turn_adds(n, t, way, z):
    return z < t - 1 if way > 0 else n - 1 - z < t - 1


def step_kernel(n, t, way, sc, recv_ref, rows_ref, w_ref, o_ref):
    adds = turn_adds(n, t, way, sc[0])

    @pl.when(adds)
    def _():
        u = dot(rows_ref[0, 0], w_ref[...])
        o_ref[0] = (recv_ref[0].astype(F32) + u).astype(BF)

    @pl.when(jnp.logical_not(adds))
    def _():
        o_ref[0] = recv_ref[0]


def step(sc, recv, rows, w, n, t, way, base):
    count, depth, hidden = recv.shape
    part = w.shape[0]
    return pl.pallas_call(
        functools.partial(step_kernel, n, t, way),
        grid_spec=pltpu.PrefetchScalarGridSpec(
            num_scalar_prefetch=1,
            grid=(count,),
            in_specs=[
                pl.BlockSpec((1, depth, hidden), lambda l, sc: (l, 0, 0)),
                pl.BlockSpec(
                    (1, 1, depth, part),
                    lambda l, sc: (turn_group(n, t, way, sc[0]), base + l, 0, 0),
                ),
                pl.BlockSpec((part, hidden), lambda l, sc: (0, base + l)),
            ],
            out_specs=pl.BlockSpec((1, depth, hidden), lambda l, sc: (l, 0, 0)),
        ),
        out_shape=jax.ShapeDtypeStruct(recv.shape, BF),
        cost_estimate=cost(
            2 * count * depth * part * hidden,
            2 * count * (2 * depth * hidden + depth * part + part * hidden),
        ),
        name="step",
    )(sc, recv, rows, w)


def last_kernel(sc, a_ref, b_ref, rows_ref, w_ref, *rest):
    u = dot(rows_ref[0, 0], w_ref[...])
    rest[-1][0] = (a_ref[0].astype(F32) + b_ref[0].astype(F32) + u).astype(BF)


def last(sc, a, b, rows, w, base, held):
    count, depth, hidden = a.shape
    part = w.shape[0]
    total = rows.shape[1]
    extra = [] if held is None else [held]
    return pl.pallas_call(
        last_kernel,
        grid_spec=pltpu.PrefetchScalarGridSpec(
            num_scalar_prefetch=1,
            grid=(count,),
            in_specs=[
                pl.BlockSpec((1, depth, hidden), lambda l, sc: (l, 0, 0)),
                pl.BlockSpec((1, depth, hidden), lambda l, sc: (l, 0, 0)),
                pl.BlockSpec((1, 1, depth, part), lambda l, sc: (sc[0], base + l, 0, 0)),
                pl.BlockSpec((part, hidden), lambda l, sc: (0, base + l)),
            ]
            + [pl.BlockSpec(memory_space=pl.ANY)] * len(extra),
            out_specs=pl.BlockSpec((1, depth, hidden), lambda l, sc: (base + l, 0, 0)),
        ),
        out_shape=jax.ShapeDtypeStruct((total, depth, hidden), BF),
        input_output_aliases={5: 0} if extra else {},
        cost_estimate=cost(
            2 * count * depth * part * hidden,
            2 * count * (3 * depth * hidden + depth * part + part * hidden),
        ),
        name="last",
    )(sc, a, b, rows, w, *extra)


def weight_kernel(n, sources, slots, base, sc, own_ref, *refs):
    others, refs = refs[: 2 * (n - 1)], refs[2 * (n - 1) :]
    rows_ref, w_ref, tgt_ref = refs[:3]
    o_ref, x_ref = refs[-2:]
    z, me = sc[0], sc[1]
    l = base + pl.program_id(0)
    depth = own_ref.shape[1]
    tokens = tgt_ref.shape[3]
    here = lax.broadcasted_iota(jnp.int32, (depth, tokens), 0).astype(F32)

    def take(h_ref, g, fresh):
        rows = rows_ref[g, 0]
        h = h_ref[0]
        grad = lax.dot_general(rows, h, (((0,), (0,)), ((), ())), preferred_element_type=F32)
        if fresh:
            o_ref[...] = grad
        else:
            o_ref[...] += grad
        u = dot(rows, w_ref[...])
        col = jnp.sum(u * h.astype(F32), axis=1, keepdims=True)
        wide = jnp.broadcast_to(col, (depth, tokens))
        for m in range(sources):
            target = tgt_ref[g, m, pl.ds(l, 1), :]
            row = jnp.sum(jnp.where(here == target, wide, 0.0), axis=0, keepdims=True)
            x_ref[0, pl.ds((me ^ m) * n + g, 1), :] = row

    take(own_ref, z, True)
    for d in range(1, n):

        @pl.when(z >= d)
        def _():
            take(others[d - 1], z - d, False)

        @pl.when(z + d < n)
        def _():
            take(others[n - 1 + d - 1], z + d, False)


def weights(sc, own, right, left, rows, w, tgt, base, held):
    n, total, depth, part = rows.shape
    count, _, hidden = right[0].shape
    _, sources, pad, tokens = tgt.shape
    extra = [] if held is None else [held]
    chunk = pl.BlockSpec((1, depth, hidden), lambda l, sc: (l, 0, 0))
    return pl.pallas_call(
        functools.partial(weight_kernel, n, sources, depth // sources, base),
        grid_spec=pltpu.PrefetchScalarGridSpec(
            num_scalar_prefetch=1,
            grid=(count,),
            in_specs=[pl.BlockSpec((1, depth, hidden), lambda l, sc: (base + l, 0, 0))]
            + [chunk] * (2 * (n - 1))
            + [
                pl.BlockSpec((n, 1, depth, part), lambda l, sc: (0, base + l, 0, 0)),
                pl.BlockSpec((part, hidden), lambda l, sc: (0, base + l)),
                pl.BlockSpec((n, sources, pad, tokens), lambda l, sc: (0, 0, 0, 0)),
            ]
            + [pl.BlockSpec(memory_space=pl.ANY)] * len(extra),
            out_specs=[
                pl.BlockSpec((part, hidden), lambda l, sc: (0, base + l)),
                pl.BlockSpec((1, sources * n, tokens), lambda l, sc: (l, 0, 0)),
            ],
        ),
        out_shape=[
            jax.ShapeDtypeStruct((part, total * hidden), F32),
            jax.ShapeDtypeStruct((count, sources * n, tokens), F32),
        ],
        input_output_aliases={2 * n + 3: 0} if extra else {},
        cost_estimate=cost(
            4 * n * count * depth * part * hidden,
            count * (2 * (2 * n - 1) * depth * hidden + 2 * n * depth * part + 6 * part * hidden),
        ),
        name="weights",
    )(sc, own, *right, *left, rows, w, tgt, *extra)


def gate_kernel(n, tokens, sc, x_ref, info_ref, o_ref, turn):
    blocks, local_experts, _ = x_ref.shape
    sources = blocks // n
    chosen = o_ref.shape[1]
    info = info_ref[0, :, :tokens].astype(F32)
    named, weights_ = info[:chosen], info[chosen : 2 * chosen]
    total = jnp.zeros((chosen, tokens), F32)
    for i in range(sources):
        both = x_ref[i * n]
        for k in range(1, n):
            both = both + x_ref[i * n + k]
        for l in range(local_experts):
            same = named == sc[2 + i * local_experts + l].astype(F32)
            total += jnp.where(same, both[l : l + 1, :], 0.0)
    turn[...] = jnp.zeros_like(turn)
    turn[:chosen] = total / weights_
    o_ref[...] = turn[...].T[:, :chosen]


def gate_grads(sc, x, packed, n, tokens, chosen):
    blocks, local_experts, _ = x.shape
    extra = packed.shape[1] - tokens
    return pl.pallas_call(
        functools.partial(gate_kernel, n, tokens),
        grid_spec=pltpu.PrefetchScalarGridSpec(
            num_scalar_prefetch=1,
            grid=(1,),
            in_specs=[
                pl.BlockSpec((blocks, local_experts, tokens), lambda i, sc: (0, 0, 0)),
                pl.BlockSpec((1, extra, packed.shape[2]), lambda i, sc: (0, tokens // extra, 0)),
            ],
            out_specs=pl.BlockSpec((tokens, chosen), lambda i, sc: (0, 0)),
            scratch_shapes=[pltpu.VMEM((tokens, tokens), F32)],
        ),
        out_shape=jax.ShapeDtypeStruct((tokens, chosen), F32),
        cost_estimate=cost(0, 4 * blocks * local_experts * tokens),
        name="gate_grads",
    )(sc, x, packed)


def local(out_grad, gates, routes, expert_slot, hidden_saved, w_down):
    tokens = out_grad.shape[1]
    chosen = routes.shape[2]
    experts = expert_slot.shape[0]
    n_ep = lax.axis_size("ep")
    n = lax.axis_size("dp")
    local_experts = experts // n_ep
    slots = hidden_saved.shape[3]
    hidden = hidden_saved.shape[4]
    depth = n_ep * slots
    z = lax.axis_index("dp").astype(jnp.int32)
    me = lax.axis_index("ep").astype(jnp.int32)
    ids = jnp.arange(experts, dtype=jnp.int32)
    expert_of = jnp.sum(jnp.where(expert_slot[None, :] == ids[:, None], ids[None, :], 0), axis=1)
    sc = jnp.concatenate([jnp.stack([z, me]), expert_of]).astype(jnp.int32)

    right = [(i, i + 1) for i in range(n - 1)]
    left = [(i + 1, i) for i in range(n - 1)]
    chunks = CHUNKS if local_experts % CHUNKS == 0 else 1
    count = local_experts // chunks
    saved = hidden_saved.reshape(local_experts, depth, hidden)

    packed = pack(out_grad[0], routes[0], gates[0], n)
    mine = lax.all_to_all(packed, "dp", split_axis=0, concat_axis=0, tiled=True)

    got_right = [[] for _ in range(chunks)]
    got_left = [[] for _ in range(chunks)]
    for c in range(chunks):
        part = lax.slice_in_dim(saved, c * count, (c + 1) * count, axis=0)
        got_right[c].append(lax.ppermute(part, "dp", right))
        got_left[c].append(lax.ppermute(part, "dp", left))

    pieces = [None] * n_ep
    pieces[0] = mine
    for m in range(2, n_ep, 2):
        pieces[m] = lax.ppermute(mine, "ep", [(e, e ^ m) for e in range(n_ep)])
    for m in range(0, n_ep, 2):
        pieces[m + 1] = lax.ppermute(pieces[m], "ep", [(e, e ^ 1) for e in range(n_ep)])

    rows, tgt = dispatch(sc, pieces, local_experts, slots, tokens, chosen)

    for t in range(2, n + 1):
        for c in range(chunks):
            a = step(sc, got_right[c][-1], rows, w_down, n, t, 1, c * count)
            got_right[c].append(lax.ppermute(a, "dp", right))
            b = step(sc, got_left[c][-1], rows, w_down, n, t, -1, c * count)
            got_left[c].append(lax.ppermute(b, "dp", left))

    weight_grad, parts = None, []
    for c in range(chunks):
        weight_grad, x = weights(
            sc,
            saved,
            got_right[c][: n - 1],
            got_left[c][: n - 1],
            rows,
            w_down,
            tgt,
            c * count,
            weight_grad,
        )
        parts.append(x)
    back = lax.all_to_all(
        jnp.concatenate(parts, axis=0).transpose(1, 0, 2),
        ("ep", "dp"),
        split_axis=0,
        concat_axis=0,
        tiled=True,
    )
    gate_grad = gate_grads(sc, back, packed, n, tokens, chosen)[None]

    hidden_grad = None
    for c in range(chunks):
        hidden_grad = last(
            sc, got_right[c][-1], got_left[c][-1], rows, w_down, c * count, hidden_grad
        )
    return (hidden_grad.reshape(hidden_saved.shape), gate_grad, weight_grad)


def solution(mesh):
    return jax.shard_map(
        local,
        mesh=mesh,
        in_specs=(
            P("dp", "ep", None),
            P("dp", "ep", None),
            P("dp", "ep", None),
            P(),
            P("dp", "ep", None, None, None),
            P("dp", "ep"),
        ),
        out_specs=(P("dp", "ep", None, None, None), P("dp", "ep", None), P("dp", "ep")),
        check_vma=False,
    )
```

```python
import functools

import jax
import jax.numpy as jnp
from jax import lax
from jax.experimental import pallas as pl
from jax.experimental.pallas import tpu as pltpu
from jax.sharding import PartitionSpec as P


BF = jnp.bfloat16
F32 = jnp.float32
CHUNKS = 2


def cost(flops, nbytes):
    return pl.CostEstimate(flops=int(flops), bytes_accessed=int(nbytes), transcendentals=0)


def dot(a, b):
    return jnp.dot(a, b, preferred_element_type=F32)


def pack_kernel(n, x_ref, r_ref, g_ref, *outs):
    chosen, tokens = r_ref.shape
    part = outs[0].shape[1]
    z = lax.axis_index("dp")
    info = jnp.concatenate([r_ref[...].astype(F32), g_ref[...].astype(F32)], axis=0).astype(BF)
    for d in range(n):
        k = lax.rem(z + d, n)
        outs[d][:tokens, :] = x_ref[:, pl.ds(pl.multiple_of(k * part, part), part)]
        outs[d][tokens:, :] = jnp.zeros((outs[d].shape[0] - tokens, part), BF)
        outs[d][tokens : tokens + 2 * chosen, :tokens] = info


def pack(x, routes, gates, n):
    tokens, width = x.shape
    chosen = routes.shape[0]
    part = width // n
    height = tokens + -(-2 * chosen // 16) * 16
    return pl.pallas_call(
        functools.partial(pack_kernel, n),
        out_shape=[jax.ShapeDtypeStruct((height, part), BF)] * n,
        cost_estimate=cost(0, 4 * tokens * width),
        name="pack",
    )(x, routes, gates)


def dispatch_kernel(dims, sc, *refs):
    sources, local_experts, slots, tokens, chosen = dims
    pieces, (rows_ref, tgt_ref), (hit, gate) = refs[:sources], refs[sources:-2], refs[-2:]
    pad = tgt_ref.shape[2]
    me = sc[1]
    line = lax.broadcasted_iota(jnp.int32, (pad, tokens), 0)
    for m in range(sources):
        info = pieces[m][0, tokens : tokens + 2 * chosen, :tokens].astype(F32)
        named, weights = info[:chosen], info[chosen:]
        hits = jnp.zeros((pad, tokens), F32)
        vals = jnp.zeros((pad, tokens), F32)
        for l in range(local_experts):
            same = named == sc[2 + me * local_experts + l].astype(F32)
            one = jnp.sum(jnp.where(same, 1.0, 0.0), axis=0, keepdims=True)
            val = jnp.sum(jnp.where(same, weights, 0.0), axis=0, keepdims=True)
            hits = jnp.where(line == l, one, hits)
            vals = jnp.where(line == l, val, vals)
        hit[m * pad : (m + 1) * pad] = hits
        gate[m * pad : (m + 1) * pad] = vals
    earlier = lax.broadcasted_iota(jnp.int32, (tokens, tokens), 0) < lax.broadcasted_iota(
        jnp.int32, (tokens, tokens), 1
    )
    rank = dot(hit[...].astype(BF), jnp.where(earlier, 1.0, 0.0).astype(BF))
    for m in range(sources):
        first = ((me ^ m) * slots).astype(F32)
        block = slice(m * pad, (m + 1) * pad)
        tgt_ref[0, m] = jnp.where(hit[block] > 0.5, rank[block] + first, -1.0)
    if slots % 16 == 0:
        place = lax.broadcasted_iota(jnp.int32, (slots, tokens), 0).astype(F32)
        for m in range(sources):
            s = me ^ m
            here = place + (s * slots).astype(F32)
            pick = [
                jnp.where(
                    here == tgt_ref[0, m, l : l + 1, :],
                    gate[m * pad + l : m * pad + l + 1, :],
                    0.0,
                ).astype(BF)
                for l in range(local_experts)
            ]
            got = dot(jnp.concatenate(pick, axis=0), pieces[m][0, :tokens, :]).astype(BF)
            for l in range(local_experts):
                rows_ref[0, l, pl.ds(pl.multiple_of(s * slots, 16), slots), :] = got[
                    l * slots : (l + 1) * slots
                ]
    else:
        here = lax.broadcasted_iota(jnp.int32, (sources * slots, tokens), 0).astype(F32)
        for l in range(local_experts):
            total = jnp.zeros((sources * slots, rows_ref.shape[3]), F32)
            for m in range(sources):
                pick = jnp.where(
                    here == tgt_ref[0, m, l : l + 1, :],
                    gate[m * pad + l : m * pad + l + 1, :],
                    0.0,
                ).astype(BF)
                total += dot(pick, pieces[m][0, :tokens, :])
            rows_ref[0, l] = total.astype(BF)


def dispatch(sc, pieces, local_experts, slots, tokens, chosen):
    sources = len(pieces)
    n, height, part = pieces[0].shape
    pad = -(-local_experts // 8) * 8
    depth = sources * slots
    return pl.pallas_call(
        functools.partial(dispatch_kernel, (sources, local_experts, slots, tokens, chosen)),
        grid_spec=pltpu.PrefetchScalarGridSpec(
            num_scalar_prefetch=1,
            grid=(n,),
            in_specs=[pl.BlockSpec((1, height, part), lambda g, sc: (g, 0, 0))] * sources,
            out_specs=[
                pl.BlockSpec((1, local_experts, depth, part), lambda d, sc: (d, 0, 0, 0)),
                pl.BlockSpec((1, sources, pad, tokens), lambda d, sc: (d, 0, 0, 0)),
            ],
            scratch_shapes=[pltpu.VMEM((sources * pad, tokens), F32)] * 2,
        ),
        out_shape=[
            jax.ShapeDtypeStruct((n, local_experts, depth, part), BF),
            jax.ShapeDtypeStruct((n, sources, pad, tokens), F32),
        ],
        cost_estimate=cost(
            2 * n * sources * local_experts * slots * tokens * part,
            2 * n * part * (sources * height + local_experts * depth),
        ),
        name="dispatch",
    )(sc, *pieces)


def turn_adds(n, t, way, z):
    return z < t - 1 if way > 0 else n - 1 - z < t - 1


def step_kernel(n, t, sc, *refs):
    recvs, rows, w_ref, outs = refs[:2], refs[2:4], refs[4], refs[5:]
    for i, way in enumerate((1, -1)):
        adds = turn_adds(n, t, way, sc[0])

        @pl.when(adds)
        def _():
            u = dot(rows[i][0, 0], w_ref[...])
            outs[i][0] = (recvs[i][0].astype(F32) + u).astype(BF)

        @pl.when(jnp.logical_not(adds))
        def _():
            outs[i][0] = recvs[i][0]


def step(sc, a, b, rows, w, n, t, base):
    count, depth, hidden = a.shape
    part = w.shape[0]
    moved = pl.BlockSpec((1, depth, hidden), lambda l, sc: (l, 0, 0))
    ahead, ahead_at = rows[t - 1]
    behind, behind_at = rows[n + 1 - t]
    return pl.pallas_call(
        functools.partial(step_kernel, n, t),
        grid_spec=pltpu.PrefetchScalarGridSpec(
            num_scalar_prefetch=1,
            grid=(count,),
            in_specs=[
                moved,
                moved,
                pl.BlockSpec((1, 1, depth, part), lambda l, sc: (ahead_at, base + l, 0, 0)),
                pl.BlockSpec((1, 1, depth, part), lambda l, sc: (behind_at, base + l, 0, 0)),
                pl.BlockSpec((part, hidden), lambda l, sc: (0, base + l)),
            ],
            out_specs=[moved, moved],
        ),
        out_shape=[jax.ShapeDtypeStruct(a.shape, BF)] * 2,
        cost_estimate=cost(
            4 * count * depth * part * hidden,
            2 * count * (4 * depth * hidden + 2 * depth * part + part * hidden),
        ),
        name="step",
    )(sc, a, b, ahead, behind, w)


def own_kernel(rows_ref, w_ref, o_ref):
    o_ref[0] = dot(rows_ref[0, 0], w_ref[...]).astype(BF)


def own_part(rows, w):
    rows, at = rows[0]
    _, total, depth, part = rows.shape
    hidden = w.shape[1] // total
    return pl.pallas_call(
        own_kernel,
        grid=(total,),
        in_specs=[
            pl.BlockSpec((1, 1, depth, part), lambda l: (at, l, 0, 0)),
            pl.BlockSpec((part, hidden), lambda l: (0, l)),
        ],
        out_specs=pl.BlockSpec((1, depth, hidden), lambda l: (l, 0, 0)),
        out_shape=jax.ShapeDtypeStruct((total, depth, hidden), BF),
        cost_estimate=cost(
            2 * total * depth * part * hidden,
            2 * total * (depth * hidden + depth * part + part * hidden),
        ),
        name="own_part",
    )(rows, w)


def weight_kernel(n, places, base, sc, own_ref, *refs):
    others, refs = refs[: 2 * (n - 1)], refs[2 * (n - 1) :]
    sets = 1 + max(p for p, _ in places)
    rows_refs, refs = refs[:sets], refs[sets:]
    tgt_refs, refs = refs[:sets], refs[sets:]
    w_ref, o_ref, x_ref = refs[0], refs[-2], refs[-1]
    z, me = sc[0], sc[1]
    l = base + pl.program_id(0)
    depth = own_ref.shape[1]
    sources, tokens = tgt_refs[0].shape[1], tgt_refs[0].shape[3]
    here = lax.broadcasted_iota(jnp.int32, (depth, tokens), 0).astype(F32)

    def take(h_ref, d, g, fresh):
        group, at = places[d]
        rows = rows_refs[group][at, 0]
        h = h_ref[0]
        grad = lax.dot_general(rows, h, (((0,), (0,)), ((), ())), preferred_element_type=F32)
        if fresh:
            o_ref[...] = grad
        else:
            o_ref[...] += grad
        u = dot(rows, w_ref[...])
        col = jnp.sum(u * h.astype(F32), axis=1, keepdims=True)
        wide = jnp.broadcast_to(col, (depth, tokens))
        for m in range(sources):
            target = tgt_refs[group][at, m, pl.ds(l, 1), :]
            row = jnp.sum(jnp.where(here == target, wide, 0.0), axis=0, keepdims=True)
            x_ref[0, pl.ds((me ^ m) * n + g, 1), :] = row

    take(own_ref, 0, z, True)
    for d in range(1, n):

        @pl.when(z >= d)
        def _():
            take(others[d - 1], d, z - d, False)

        @pl.when(z + d < n)
        def _():
            take(others[n - 1 + d - 1], n - d, z + d, False)


def weights(sc, own, right, left, sets, places, w, base, held):
    n = len(places)
    _, total, depth, part = sets[0][0].shape
    count, _, hidden = right[0].shape
    _, sources, _, tokens = sets[0][1].shape
    extra = [] if held is None else [held]
    chunk = pl.BlockSpec((1, depth, hidden), lambda l, sc: (l, 0, 0))
    return pl.pallas_call(
        functools.partial(weight_kernel, n, places, base),
        grid_spec=pltpu.PrefetchScalarGridSpec(
            num_scalar_prefetch=1,
            grid=(count,),
            in_specs=[pl.BlockSpec((1, depth, hidden), lambda l, sc: (base + l, 0, 0))]
            + [chunk] * (2 * (n - 1))
            + [
                pl.BlockSpec((rows.shape[0], 1, depth, part), lambda l, sc: (0, base + l, 0, 0))
                for rows, _ in sets
            ]
            + [pl.BlockSpec(tgt.shape, lambda l, sc: (0, 0, 0, 0)) for _, tgt in sets]
            + [pl.BlockSpec((part, hidden), lambda l, sc: (0, base + l))]
            + [pl.BlockSpec(memory_space=pl.ANY)] * len(extra),
            out_specs=[
                pl.BlockSpec((part, hidden), lambda l, sc: (0, base + l)),
                pl.BlockSpec((1, sources * n, tokens), lambda l, sc: (l, 0, 0)),
            ],
        ),
        out_shape=[
            jax.ShapeDtypeStruct((part, total * hidden), F32),
            jax.ShapeDtypeStruct((count, sources * n, tokens), F32),
        ],
        input_output_aliases={2 * n + 2 * len(sets) + 1: 0} if extra else {},
        cost_estimate=cost(
            4 * n * count * depth * part * hidden,
            count * (2 * (2 * n - 1) * depth * hidden + 2 * n * depth * part + 6 * part * hidden),
        ),
        name="weights",
    )(sc, own, *right, *left, *[r for r, _ in sets], *[t for _, t in sets], w, *extra)


def gate_kernel(n, tokens, sc, x_ref, info_ref, o_ref):
    blocks, local_experts, _ = x_ref.shape
    sources = blocks // n
    chosen = o_ref.shape[0]
    info = info_ref[:, :tokens].astype(F32)
    named, shares = info[:chosen], info[chosen : 2 * chosen]
    total = jnp.zeros((chosen, tokens), F32)
    for i in range(sources):
        both = x_ref[i * n]
        for k in range(1, n):
            both = both + x_ref[i * n + k]
        for l in range(local_experts):
            same = named == sc[2 + i * local_experts + l].astype(F32)
            total += jnp.where(same, both[l : l + 1, :], 0.0)
    o_ref[...] = total / shares


def gate_grads(sc, x, packed, n, tokens, chosen):
    blocks, local_experts, _ = x.shape
    extra = packed.shape[0] - tokens
    return pl.pallas_call(
        functools.partial(gate_kernel, n, tokens),
        grid_spec=pltpu.PrefetchScalarGridSpec(
            num_scalar_prefetch=1,
            grid=(1,),
            in_specs=[
                pl.BlockSpec((blocks, local_experts, tokens), lambda i, sc: (0, 0, 0)),
                pl.BlockSpec((extra, packed.shape[1]), lambda i, sc: (tokens // extra, 0)),
            ],
            out_specs=pl.BlockSpec((chosen, tokens), lambda i, sc: (0, 0)),
        ),
        out_shape=jax.ShapeDtypeStruct((chosen, tokens), F32),
        cost_estimate=cost(0, 4 * blocks * local_experts * tokens),
        name="gate_grads",
    )(sc, x, packed)


def local(out_grad, gates, routes, expert_slot, hidden_saved, w_down):
    tokens = out_grad.shape[1]
    chosen = routes.shape[2]
    experts = expert_slot.shape[0]
    n_ep = lax.axis_size("ep")
    n = lax.axis_size("dp")
    local_experts = experts // n_ep
    slots = hidden_saved.shape[3]
    hidden = hidden_saved.shape[4]
    depth = n_ep * slots
    z = lax.axis_index("dp").astype(jnp.int32)
    me = lax.axis_index("ep").astype(jnp.int32)
    ids = jnp.arange(experts, dtype=jnp.int32)
    expert_of = jnp.sum(jnp.where(expert_slot[None, :] == ids[:, None], ids[None, :], 0), axis=1)
    sc = jnp.concatenate([jnp.stack([z, me]), expert_of]).astype(jnp.int32)

    right = [(i, i + 1) for i in range(n - 1)]
    left = [(i + 1, i) for i in range(n - 1)]
    chunks = CHUNKS if local_experts % CHUNKS == 0 else 1
    count = local_experts // chunks
    saved = hidden_saved.reshape(local_experts, depth, hidden)

    packed = pack(out_grad[0], routes[0].T, gates[0].T, n)
    saved, packed = lax.optimization_barrier((saved, packed))
    arrived = [packed[0]]
    for d in range(1, n):
        arrived.append(lax.ppermute(packed[d], "dp", [(i, (i + d) % n) for i in range(n)]))

    got_right = [[] for _ in range(chunks)]
    got_left = [[] for _ in range(chunks)]
    source = saved
    for c in range(chunks):
        if c > 0:
            source, arrived[1] = lax.optimization_barrier((source, arrived[1]))
        part = lax.slice_in_dim(source, c * count, (c + 1) * count, axis=0)
        got_right[c].append(lax.ppermute(part, "dp", right))
        got_left[c].append(lax.ppermute(part, "dp", left))

    first = sorted({1, n - 1})
    orders = [first, [d for d in range(n) if d not in first]]
    places = [None] * n
    sets = []
    for i, order in enumerate(orders):
        for at, d in enumerate(order):
            places[d] = (i, at)
        pieces = [jnp.stack([arrived[d] for d in order])] + [None] * (n_ep - 1)
        for m in range(2, n_ep, 2):
            pieces[m] = lax.ppermute(pieces[0], "ep", [(e, e ^ m) for e in range(n_ep)])
        for m in range(0, n_ep, 2):
            pieces[m + 1] = lax.ppermute(pieces[m], "ep", [(e, e ^ 1) for e in range(n_ep)])
        sets.append(dispatch(sc, pieces, local_experts, slots, tokens, chosen))
    rows = [(sets[i][0], at) for i, at in places]
    own = own_part(rows, w_down)

    weight_grad, parts = None, []
    for t in range(2, n + 1):
        for c in range(chunks):
            base = c * count
            a, b = got_right[c][-1], got_left[c][-1]
            if t == n and c > 0:
                a, b, weight_grad = lax.optimization_barrier((a, b, weight_grad))
            a, b = step(sc, a, b, rows, w_down, n, t, base)
            got_right[c].append(lax.ppermute(a, "dp", right))
            got_left[c].append(lax.ppermute(b, "dp", left))
            if t == n:
                weight_grad, x = weights(
                    sc,
                    saved,
                    got_right[c][: n - 1],
                    got_left[c][: n - 1],
                    sets,
                    places,
                    w_down,
                    base,
                    weight_grad,
                )
                parts.append(x)
    hidden_grad = own
    ready = jnp.concatenate(parts, axis=0).transpose(1, 0, 2)
    for c in range(chunks):
        mine = lax.slice_in_dim(own, c * count, (c + 1) * count, axis=0).astype(F32)
        total = mine + got_right[c][-1].astype(F32) + got_left[c][-1].astype(F32)
        hidden_grad = lax.dynamic_update_slice_in_dim(
            hidden_grad, total.astype(BF), c * count, axis=0
        )
        if c < chunks - 1:
            hidden_grad, ready = lax.optimization_barrier((hidden_grad, ready))
            own = hidden_grad
    back = lax.all_to_all(ready, ("ep", "dp"), split_axis=0, concat_axis=0, tiled=True)
    gate_grad = gate_grads(sc, back, packed[0], n, tokens, chosen).T[None]
    return (hidden_grad.reshape(hidden_saved.shape), gate_grad, weight_grad)


def solution(mesh):
    return jax.shard_map(
        local,
        mesh=mesh,
        in_specs=(
            P("dp", "ep", None),
            P("dp", "ep", None),
            P("dp", "ep", None),
            P(),
            P("dp", "ep", None, None, None),
            P("dp", "ep"),
        ),
        out_specs=(P("dp", "ep", None, None, None), P("dp", "ep", None), P("dp", "ep")),
        check_vma=False,
    )
```

```python
import functools

import jax
import jax.numpy as jnp
from jax import lax
from jax.experimental import pallas as pl
from jax.experimental.pallas import tpu as pltpu
from jax.sharding import PartitionSpec as P


BF = jnp.bfloat16
F32 = jnp.float32
CHUNKS = 2


def cost(flops, nbytes):
    return pl.CostEstimate(flops=int(flops), bytes_accessed=int(nbytes), transcendentals=0)


def dot(a, b):
    return jnp.dot(a, b, preferred_element_type=F32)


def pack_kernel(n, x_ref, r_ref, g_ref, *outs):
    chosen, tokens = r_ref.shape
    part = outs[0].shape[1]
    z = lax.axis_index("dp")
    for d in range(n):
        k = lax.rem(z + d, n)
        outs[d][:tokens, :] = x_ref[:, pl.ds(pl.multiple_of(k * part, part), part)]
        outs[d][tokens:, :] = jnp.zeros((outs[d].shape[0] - tokens, part), BF)
        outs[d][tokens : tokens + chosen, :tokens] = r_ref[...].astype(F32).astype(BF)
        outs[d][tokens : tokens + chosen, tokens : 2 * tokens] = g_ref[...]


def pack(x, routes, gates, n):
    tokens, width = x.shape
    chosen = routes.shape[0]
    part = width // n
    height = tokens + -(-chosen // 8) * 8
    return pl.pallas_call(
        functools.partial(pack_kernel, n),
        out_shape=[jax.ShapeDtypeStruct((height, part), BF)] * n,
        cost_estimate=cost(0, 4 * tokens * width),
        name="pack",
    )(x, routes, gates)


def dispatch_kernel(dims, sc, *refs):
    sources, local_experts, slots, tokens, chosen = dims
    pieces, (rows_ref, tgt_ref), (hit, gate) = refs[:sources], refs[sources:-2], refs[-2:]
    pad = tgt_ref.shape[2]
    me = sc[1]
    line = lax.broadcasted_iota(jnp.int32, (pad, tokens), 0)
    for m in range(sources):
        named = pieces[m][0, tokens : tokens + chosen, :tokens].astype(F32)
        weights = pieces[m][0, tokens : tokens + chosen, tokens : 2 * tokens].astype(F32)
        hits = jnp.zeros((pad, tokens), F32)
        vals = jnp.zeros((pad, tokens), F32)
        for l in range(local_experts):
            same = named == sc[2 + me * local_experts + l].astype(F32)
            one = jnp.sum(jnp.where(same, 1.0, 0.0), axis=0, keepdims=True)
            val = jnp.sum(jnp.where(same, weights, 0.0), axis=0, keepdims=True)
            hits = jnp.where(line == l, one, hits)
            vals = jnp.where(line == l, val, vals)
        hit[m * pad : (m + 1) * pad] = hits
        gate[m * pad : (m + 1) * pad] = vals
    earlier = lax.broadcasted_iota(jnp.int32, (tokens, tokens), 0) < lax.broadcasted_iota(
        jnp.int32, (tokens, tokens), 1
    )
    rank = dot(hit[...].astype(BF), jnp.where(earlier, 1.0, 0.0).astype(BF))
    for m in range(sources):
        first = ((me ^ m) * slots).astype(F32)
        block = slice(m * pad, (m + 1) * pad)
        tgt_ref[0, m] = jnp.where(hit[block] > 0.5, rank[block] + first, -1.0)
    if slots % 16 == 0:
        place = lax.broadcasted_iota(jnp.int32, (slots, tokens), 0).astype(F32)
        for m in range(sources):
            s = me ^ m
            here = place + (s * slots).astype(F32)
            pick = [
                jnp.where(
                    here == tgt_ref[0, m, l : l + 1, :],
                    gate[m * pad + l : m * pad + l + 1, :],
                    0.0,
                ).astype(BF)
                for l in range(local_experts)
            ]
            got = dot(jnp.concatenate(pick, axis=0), pieces[m][0, :tokens, :]).astype(BF)
            for l in range(local_experts):
                rows_ref[0, l, pl.ds(pl.multiple_of(s * slots, 16), slots), :] = got[
                    l * slots : (l + 1) * slots
                ]
    else:
        here = lax.broadcasted_iota(jnp.int32, (sources * slots, tokens), 0).astype(F32)
        for l in range(local_experts):
            total = jnp.zeros((sources * slots, rows_ref.shape[3]), F32)
            for m in range(sources):
                pick = jnp.where(
                    here == tgt_ref[0, m, l : l + 1, :],
                    gate[m * pad + l : m * pad + l + 1, :],
                    0.0,
                ).astype(BF)
                total += dot(pick, pieces[m][0, :tokens, :])
            rows_ref[0, l] = total.astype(BF)


def dispatch(sc, pieces, local_experts, slots, tokens, chosen):
    sources = len(pieces)
    n, height, part = pieces[0].shape
    pad = -(-local_experts // 8) * 8
    depth = sources * slots
    return pl.pallas_call(
        functools.partial(dispatch_kernel, (sources, local_experts, slots, tokens, chosen)),
        grid_spec=pltpu.PrefetchScalarGridSpec(
            num_scalar_prefetch=1,
            grid=(n,),
            in_specs=[pl.BlockSpec((1, height, part), lambda g, sc: (g, 0, 0))] * sources,
            out_specs=[
                pl.BlockSpec((1, local_experts, depth, part), lambda d, sc: (d, 0, 0, 0)),
                pl.BlockSpec((1, sources, pad, tokens), lambda d, sc: (d, 0, 0, 0)),
            ],
            scratch_shapes=[pltpu.VMEM((sources * pad, tokens), F32)] * 2,
        ),
        out_shape=[
            jax.ShapeDtypeStruct((n, local_experts, depth, part), BF),
            jax.ShapeDtypeStruct((n, sources, pad, tokens), F32),
        ],
        cost_estimate=cost(
            2 * n * sources * local_experts * slots * tokens * part,
            2 * n * part * (sources * height + local_experts * depth),
        ),
        name="dispatch",
    )(sc, *pieces)


def heading(z, n, i):
    odd = lax.rem(z, 2)
    up = 1 - odd if i == 0 else odd
    return up, up * z + (1 - up) * (n - 1 - z)


def step_kernel(n, t, sc, *refs):
    recvs, rows, w_ref, outs = refs[:2], refs[2:4], refs[4], refs[5:]
    for i in range(2):
        adds = heading(sc[0], n, i)[1] < t - 1

        @pl.when(adds)
        def _():
            u = dot(rows[i][0, 0], w_ref[...])
            outs[i][0] = (recvs[i][0].astype(F32) + u).astype(BF)

        @pl.when(jnp.logical_not(adds))
        def _():
            outs[i][0] = recvs[i][0]


def step(sc, a, b, rows, w, n, t, base):
    count, depth, hidden = a.shape
    part = w.shape[0]
    moved = pl.BlockSpec((1, depth, hidden), lambda l, sc: (l, 0, 0))
    source, up_at = rows[t - 1]
    _, down_at = rows[n + 1 - t]

    def block(i):
        def at(l, sc):
            up = heading(sc[0], n, i)[0]
            return up * up_at + (1 - up) * down_at, base + l, 0, 0

        return pl.BlockSpec((1, 1, depth, part), at)

    return pl.pallas_call(
        functools.partial(step_kernel, n, t),
        grid_spec=pltpu.PrefetchScalarGridSpec(
            num_scalar_prefetch=1,
            grid=(count,),
            in_specs=[
                moved,
                moved,
                block(0),
                block(1),
                pl.BlockSpec((part, hidden), lambda l, sc: (0, base + l)),
            ],
            out_specs=[moved, moved],
        ),
        out_shape=[jax.ShapeDtypeStruct(a.shape, BF)] * 2,
        cost_estimate=cost(
            4 * count * depth * part * hidden,
            2 * count * (4 * depth * hidden + 2 * depth * part + part * hidden),
        ),
        name="step",
    )(sc, a, b, source, source, w)


def own_kernel(rows_ref, w_ref, o_ref):
    o_ref[0] = dot(rows_ref[0, 0], w_ref[...]).astype(BF)


def own_part(rows, w):
    rows, at = rows[0]
    _, total, depth, part = rows.shape
    hidden = w.shape[1] // total
    return pl.pallas_call(
        own_kernel,
        grid=(total,),
        in_specs=[
            pl.BlockSpec((1, 1, depth, part), lambda l: (at, l, 0, 0)),
            pl.BlockSpec((part, hidden), lambda l: (0, l)),
        ],
        out_specs=pl.BlockSpec((1, depth, hidden), lambda l: (l, 0, 0)),
        out_shape=jax.ShapeDtypeStruct((total, depth, hidden), BF),
        cost_estimate=cost(
            2 * total * depth * part * hidden,
            2 * total * (depth * hidden + depth * part + part * hidden),
        ),
        name="own_part",
    )(rows, w)


def weight_kernel(n, places, base, sc, own_ref, *refs):
    others, refs = refs[: 2 * (n - 1)], refs[2 * (n - 1) :]
    sets = 1 + max(p for p, _ in places)
    rows_refs, refs = refs[:sets], refs[sets:]
    tgt_refs, refs = refs[:sets], refs[sets:]
    w_ref, o_ref, x_ref = refs[0], refs[-2], refs[-1]
    z, me = sc[0], sc[1]
    l = base + pl.program_id(0)
    depth = own_ref.shape[1]
    sources, tokens = tgt_refs[0].shape[1], tgt_refs[0].shape[3]
    here = lax.broadcasted_iota(jnp.int32, (depth, tokens), 0).astype(F32)

    def take(h_ref, place, g, fresh):
        group, at = place
        rows = rows_refs[group][at, 0]
        h = h_ref[0]
        grad = lax.dot_general(rows, h, (((0,), (0,)), ((), ())), preferred_element_type=F32)
        if fresh:
            o_ref[...] = grad
        else:
            o_ref[...] += grad
        u = dot(rows, w_ref[...])
        col = jnp.sum(u * h.astype(F32), axis=1, keepdims=True)
        wide = jnp.broadcast_to(col, (depth, tokens))
        for m in range(sources):
            target = tgt_refs[group][at, m, pl.ds(l, 1), :]
            row = jnp.sum(jnp.where(here == target, wide, 0.0), axis=0, keepdims=True)
            x_ref[0, pl.ds((me ^ m) * n + g, 1), :] = row

    take(own_ref, places[0], z, True)
    for d in range(1, n):
        for i in range(2):
            up, behind = heading(z, n, i)
            place = (places[d][0], up * places[d][1] + (1 - up) * places[n - d][1])

            @pl.when(behind >= d)
            def _():
                take(others[i * (n - 1) + d - 1], place, z + d * (1 - 2 * up), False)


def weights(sc, own, one, two, sets, places, w, base, held):
    n = len(places)
    _, total, depth, part = sets[0][0].shape
    count, _, hidden = one[0].shape
    _, sources, _, tokens = sets[0][1].shape
    extra = [] if held is None else [held]
    chunk = pl.BlockSpec((1, depth, hidden), lambda l, sc: (l, 0, 0))
    return pl.pallas_call(
        functools.partial(weight_kernel, n, places, base),
        grid_spec=pltpu.PrefetchScalarGridSpec(
            num_scalar_prefetch=1,
            grid=(count,),
            in_specs=[pl.BlockSpec((1, depth, hidden), lambda l, sc: (base + l, 0, 0))]
            + [chunk] * (2 * (n - 1))
            + [
                pl.BlockSpec((rows.shape[0], 1, depth, part), lambda l, sc: (0, base + l, 0, 0))
                for rows, _ in sets
            ]
            + [pl.BlockSpec(tgt.shape, lambda l, sc: (0, 0, 0, 0)) for _, tgt in sets]
            + [pl.BlockSpec((part, hidden), lambda l, sc: (0, base + l))]
            + [pl.BlockSpec(memory_space=pl.ANY)] * len(extra),
            out_specs=[
                pl.BlockSpec((part, hidden), lambda l, sc: (0, base + l)),
                pl.BlockSpec((1, sources * n, tokens), lambda l, sc: (l, 0, 0)),
            ],
        ),
        out_shape=[
            jax.ShapeDtypeStruct((part, total * hidden), F32),
            jax.ShapeDtypeStruct((count, sources * n, tokens), F32),
        ],
        input_output_aliases={2 * n + 2 * len(sets) + 1: 0} if extra else {},
        cost_estimate=cost(
            4 * n * count * depth * part * hidden,
            count * (2 * (2 * n - 1) * depth * hidden + 2 * n * depth * part + 6 * part * hidden),
        ),
        name="weights",
    )(sc, own, *one, *two, *[r for r, _ in sets], *[t for _, t in sets], w, *extra)


def shares(expert_of, routes, gates, n_ep):
    ids = expert_of.reshape(n_ep, 1, -1, 1, 1)
    mine = routes[None, None, None] == ids
    return jnp.where(mine, 1.0 / gates.astype(F32), 0.0)


def local(out_grad, gates, routes, expert_slot, hidden_saved, w_down):
    tokens = out_grad.shape[1]
    chosen = routes.shape[2]
    experts = expert_slot.shape[0]
    n_ep = lax.axis_size("ep")
    n = lax.axis_size("dp")
    local_experts = experts // n_ep
    slots = hidden_saved.shape[3]
    hidden = hidden_saved.shape[4]
    depth = n_ep * slots
    z = lax.axis_index("dp").astype(jnp.int32)
    me = lax.axis_index("ep").astype(jnp.int32)
    ids = jnp.arange(experts, dtype=jnp.int32)
    expert_of = jnp.sum(jnp.where(expert_slot[None, :] == ids[:, None], ids[None, :], 0), axis=1)
    sc = jnp.concatenate([jnp.stack([z, me]), expert_of]).astype(jnp.int32)

    swaps = []
    for start in (1, 0):
        pairs = [(i, i + 1) for i in range(start, n - 1, 2)]
        swaps.append(pairs + [(j, i) for i, j in pairs])
    chunks = CHUNKS if local_experts % CHUNKS == 0 else 1
    count = local_experts // chunks
    saved = hidden_saved.reshape(local_experts, depth, hidden)

    packed = pack(out_grad[0], routes[0].T, gates[0].T, n)
    saved, packed = lax.optimization_barrier((saved, packed))
    first = sorted({1, n - 1})
    orders = [first, [d for d in range(n) if d not in first]]
    arrived = list(packed)
    for order in orders:
        for d in order:
            if d > 0:
                shift = [(j, (j + d) % n) for j in range(n)]
                arrived[d] = lax.ppermute(packed[d], "dp", shift)

    got = [[[], []] for _ in range(chunks)]
    source = saved
    for c in range(chunks):
        if c > 0:
            source, arrived[1] = lax.optimization_barrier((source, arrived[1]))
        part = lax.slice_in_dim(source, c * count, (c + 1) * count, axis=0)
        for i in range(2):
            got[c][i].append(lax.ppermute(part, "dp", swaps[i]))

    places = [None] * n
    sets = []
    for i, order in enumerate(orders):
        for at, d in enumerate(order):
            places[d] = (i, at)
        pieces = [jnp.stack([arrived[d] for d in order])] + [None] * (n_ep - 1)
        for m in range(2, n_ep, 2):
            pieces[m] = lax.ppermute(pieces[0], "ep", [(e, e ^ m) for e in range(n_ep)])
        for m in range(0, n_ep, 2):
            pieces[m + 1] = lax.ppermute(pieces[m], "ep", [(e, e ^ 1) for e in range(n_ep)])
        sets.append(dispatch(sc, pieces, local_experts, slots, tokens, chosen))
    rows = [(sets[i][0], at) for i, at in places]
    own = own_part(rows, w_down)

    weight_grad, parts = None, []
    for t in range(2, n + 1):
        for c in range(chunks):
            base = c * count
            a, b = got[c][0][-1], got[c][1][-1]
            if t == n and c == 0:
                a, b, own = lax.optimization_barrier((a, b, own))
            if t == n and c > 0:
                a, b, weight_grad = lax.optimization_barrier((a, b, weight_grad))
            a, b = step(sc, a, b, rows, w_down, n, t, base)
            got[c][1].append(lax.ppermute(a, "dp", swaps[1]))
            got[c][0].append(lax.ppermute(b, "dp", swaps[0]))
            if t == n:
                weight_grad, x = weights(
                    sc,
                    saved,
                    got[c][0][: n - 1],
                    got[c][1][: n - 1],
                    sets,
                    places,
                    w_down,
                    base,
                    weight_grad,
                )
                parts.append(x)
    ready = jnp.concatenate(parts, axis=0).transpose(1, 0, 2)
    for c in range(chunks):
        base = c * count
        if c < chunks - 1:
            total = lax.slice_in_dim(own, base, base + count, axis=0).astype(F32)
            for part in got[c]:
                total = total + part[-1].astype(F32)
            own = lax.dynamic_update_slice_in_dim(own, total.astype(BF), base, axis=0)
            own, ready = lax.optimization_barrier((own, ready))
    inverse = shares(expert_of, routes[0].T, gates[0].T, n_ep)
    ready, inverse = lax.optimization_barrier((ready, inverse))
    back = lax.all_to_all(ready, ("ep", "dp"), split_axis=0, concat_axis=0, tiled=True)
    total = own.astype(F32)
    for part in got[-1]:
        wide = ((local_experts - count, 0), (0, 0), (0, 0))
        total = total + jnp.pad(part[-1], wide).astype(F32)
    hidden_grad = total.astype(BF)
    back, hidden_grad = lax.optimization_barrier((back, hidden_grad))
    back = back.reshape(n_ep, n, local_experts, 1, tokens)
    gate_grad = jnp.sum(back * inverse, axis=(0, 1, 2)).T[None]
    return (hidden_grad.reshape(hidden_saved.shape), gate_grad, weight_grad)


def solution(mesh):
    return jax.shard_map(
        local,
        mesh=mesh,
        in_specs=(
            P("dp", "ep", None),
            P("dp", "ep", None),
            P("dp", "ep", None),
            P(),
            P("dp", "ep", None, None, None),
            P("dp", "ep"),
        ),
        out_specs=(P("dp", "ep", None, None, None), P("dp", "ep", None), P("dp", "ep")),
        check_vma=False,
    )
```

```python
import functools

import jax
import jax.numpy as jnp
from jax import lax
from jax.experimental import pallas as pl
from jax.experimental.pallas import tpu as pltpu
from jax.sharding import PartitionSpec as P


BF = jnp.bfloat16
F32 = jnp.float32
CHUNKS = 2


def cost(flops, nbytes):
    return pl.CostEstimate(flops=int(flops), bytes_accessed=int(nbytes), transcendentals=0)


def dot(a, b):
    return jnp.dot(a, b, preferred_element_type=F32)


def pack_kernel(n, x_ref, r_ref, g_ref, *outs):
    chosen, tokens = r_ref.shape
    part = outs[0].shape[1]
    z = lax.axis_index("dp")
    for d in range(n):
        k = lax.rem(z + d, n)
        outs[d][:tokens, :] = x_ref[:, pl.ds(pl.multiple_of(k * part, part), part)]
        outs[d][tokens:, :] = jnp.zeros((outs[d].shape[0] - tokens, part), BF)
        outs[d][tokens : tokens + chosen, :tokens] = r_ref[...].astype(F32).astype(BF)
        outs[d][tokens : tokens + chosen, tokens : 2 * tokens] = g_ref[...]


def pack(x, routes, gates, n):
    tokens, width = x.shape
    chosen = routes.shape[0]
    part = width // n
    height = tokens + -(-chosen // 8) * 8
    return pl.pallas_call(
        functools.partial(pack_kernel, n),
        out_shape=[jax.ShapeDtypeStruct((height, part), BF)] * n,
        cost_estimate=cost(0, 4 * tokens * width),
        name="pack",
    )(x, routes, gates)


def dispatch_kernel(dims, sc, *refs):
    sources, local_experts, slots, tokens, chosen = dims
    pieces, (rows_ref, tgt_ref), (hit, gate) = refs[:sources], refs[sources:-2], refs[-2:]
    pad = tgt_ref.shape[2]
    me = sc[1]
    line = lax.broadcasted_iota(jnp.int32, (pad, tokens), 0)
    for m in range(sources):
        named = pieces[m][0, tokens : tokens + chosen, :tokens].astype(F32)
        weights = pieces[m][0, tokens : tokens + chosen, tokens : 2 * tokens].astype(F32)
        hits = jnp.zeros((pad, tokens), F32)
        vals = jnp.zeros((pad, tokens), F32)
        for l in range(local_experts):
            same = named == sc[2 + me * local_experts + l].astype(F32)
            one = jnp.sum(jnp.where(same, 1.0, 0.0), axis=0, keepdims=True)
            val = jnp.sum(jnp.where(same, weights, 0.0), axis=0, keepdims=True)
            hits = jnp.where(line == l, one, hits)
            vals = jnp.where(line == l, val, vals)
        hit[m * pad : (m + 1) * pad] = hits
        gate[m * pad : (m + 1) * pad] = vals
    earlier = lax.broadcasted_iota(jnp.int32, (tokens, tokens), 0) < lax.broadcasted_iota(
        jnp.int32, (tokens, tokens), 1
    )
    rank = dot(hit[...].astype(BF), jnp.where(earlier, 1.0, 0.0).astype(BF))
    for m in range(sources):
        first = ((me ^ m) * slots).astype(F32)
        block = slice(m * pad, (m + 1) * pad)
        tgt_ref[0, m] = jnp.where(hit[block] > 0.5, rank[block] + first, -1.0)
    if slots % 16 == 0:
        place = lax.broadcasted_iota(jnp.int32, (slots, tokens), 0).astype(F32)
        for m in range(sources):
            s = me ^ m
            here = place + (s * slots).astype(F32)
            pick = [
                jnp.where(
                    here == tgt_ref[0, m, l : l + 1, :],
                    gate[m * pad + l : m * pad + l + 1, :],
                    0.0,
                ).astype(BF)
                for l in range(local_experts)
            ]
            got = dot(jnp.concatenate(pick, axis=0), pieces[m][0, :tokens, :]).astype(BF)
            for l in range(local_experts):
                rows_ref[0, l, pl.ds(pl.multiple_of(s * slots, 16), slots), :] = got[
                    l * slots : (l + 1) * slots
                ]
    else:
        here = lax.broadcasted_iota(jnp.int32, (sources * slots, tokens), 0).astype(F32)
        for l in range(local_experts):
            total = jnp.zeros((sources * slots, rows_ref.shape[3]), F32)
            for m in range(sources):
                pick = jnp.where(
                    here == tgt_ref[0, m, l : l + 1, :],
                    gate[m * pad + l : m * pad + l + 1, :],
                    0.0,
                ).astype(BF)
                total += dot(pick, pieces[m][0, :tokens, :])
            rows_ref[0, l] = total.astype(BF)


def dispatch(sc, pieces, local_experts, slots, tokens, chosen):
    sources = len(pieces)
    n, height, part = pieces[0].shape
    pad = -(-local_experts // 8) * 8
    depth = sources * slots
    return pl.pallas_call(
        functools.partial(dispatch_kernel, (sources, local_experts, slots, tokens, chosen)),
        grid_spec=pltpu.PrefetchScalarGridSpec(
            num_scalar_prefetch=1,
            grid=(n,),
            in_specs=[pl.BlockSpec((1, height, part), lambda g, sc: (g, 0, 0))] * sources,
            out_specs=[
                pl.BlockSpec((1, local_experts, depth, part), lambda d, sc: (d, 0, 0, 0)),
                pl.BlockSpec((1, sources, pad, tokens), lambda d, sc: (d, 0, 0, 0)),
            ],
            scratch_shapes=[pltpu.VMEM((sources * pad, tokens), F32)] * 2,
        ),
        out_shape=[
            jax.ShapeDtypeStruct((n, local_experts, depth, part), BF),
            jax.ShapeDtypeStruct((n, sources, pad, tokens), F32),
        ],
        cost_estimate=cost(
            2 * n * sources * local_experts * slots * tokens * part,
            2 * n * part * (sources * height + local_experts * depth),
        ),
        name="dispatch",
    )(sc, *pieces)


def heading(z, n, i):
    odd = lax.rem(z, 2)
    up = 1 - odd if i == 0 else odd
    return up, up * z + (1 - up) * (n - 1 - z)


def step_kernel(n, t, sc, *refs):
    recvs, rows, w_ref, outs = refs[:2], refs[2:4], refs[4], refs[5:]
    for i in range(2):
        adds = heading(sc[0], n, i)[1] < t - 1

        @pl.when(adds)
        def _():
            u = dot(rows[i][0, 0], w_ref[...])
            outs[i][0] = (recvs[i][0].astype(F32) + u).astype(BF)

        @pl.when(jnp.logical_not(adds))
        def _():
            outs[i][0] = recvs[i][0]


def step(sc, a, b, rows, w, n, t, base):
    count, depth, hidden = a.shape
    part = w.shape[0]
    moved = pl.BlockSpec((1, depth, hidden), lambda l, sc: (l, 0, 0))
    source, up_at = rows[t - 1]
    _, down_at = rows[n + 1 - t]

    def block(i):
        def at(l, sc):
            up = heading(sc[0], n, i)[0]
            return up * up_at + (1 - up) * down_at, base + l, 0, 0

        return pl.BlockSpec((1, 1, depth, part), at)

    return pl.pallas_call(
        functools.partial(step_kernel, n, t),
        grid_spec=pltpu.PrefetchScalarGridSpec(
            num_scalar_prefetch=1,
            grid=(count,),
            in_specs=[
                moved,
                moved,
                block(0),
                block(1),
                pl.BlockSpec((part, hidden), lambda l, sc: (0, base + l)),
            ],
            out_specs=[moved, moved],
        ),
        out_shape=[jax.ShapeDtypeStruct(a.shape, BF)] * 2,
        cost_estimate=cost(
            4 * count * depth * part * hidden,
            2 * count * (4 * depth * hidden + 2 * depth * part + part * hidden),
        ),
        name="step",
    )(sc, a, b, source, source, w)


def own_kernel(rows_ref, w_ref, o_ref):
    o_ref[0] = dot(rows_ref[0, 0], w_ref[...]).astype(BF)


def own_part(rows, w):
    rows, at = rows[0]
    _, total, depth, part = rows.shape
    hidden = w.shape[1] // total
    return pl.pallas_call(
        own_kernel,
        grid=(total,),
        in_specs=[
            pl.BlockSpec((1, 1, depth, part), lambda l: (at, l, 0, 0)),
            pl.BlockSpec((part, hidden), lambda l: (0, l)),
        ],
        out_specs=pl.BlockSpec((1, depth, hidden), lambda l: (l, 0, 0)),
        out_shape=jax.ShapeDtypeStruct((total, depth, hidden), BF),
        cost_estimate=cost(
            2 * total * depth * part * hidden,
            2 * total * (depth * hidden + depth * part + part * hidden),
        ),
        name="own_part",
    )(rows, w)


def arrivals(n, d):
    found = []
    for i in range(2):
        for z in range(n):
            up = 1 - z % 2 if i == 0 else z % 2
            if (z if up else n - 1 - z) >= d and i not in found:
                found.append(i)
    return found


def weight_kernel(n, places, base, pairs, mode, sc, *refs):
    refs = list(refs)
    sets = 1 + max(p for p, _ in places)
    own_ref = refs.pop(0) if mode == "begin" else None
    others = [refs.pop(0) for _ in pairs]
    rows_refs = [refs.pop(0) for _ in range(sets)]
    if mode != "end":
        tgt_refs = [refs.pop(0) for _ in range(sets)]
        w_ref = refs.pop(0)
        x_ref = refs[-1]
        sources, tokens = tgt_refs[0].shape[1], tgt_refs[0].shape[3]
    o_ref = {"begin": refs[-2], "parts": None, "end": refs[-1]}[mode]
    z, me = sc[0], sc[1]
    l = base + pl.program_id(0)
    depth = rows_refs[0].shape[2]
    if mode != "begin":
        refs[-1][...] = refs[0][...]

    def take(h_ref, place, g, fresh):
        group, at = place
        rows = rows_refs[group][at, 0]
        h = h_ref[0]
        if mode != "parts":
            grad = lax.dot_general(rows, h, (((0,), (0,)), ((), ())), preferred_element_type=F32)
            if fresh:
                o_ref[...] = grad
            else:
                o_ref[...] += grad
        if mode != "end":
            here = lax.broadcasted_iota(jnp.int32, (depth, tokens), 0).astype(F32)
            u = dot(rows, w_ref[...])
            col = jnp.sum(u * h.astype(F32), axis=1, keepdims=True)
            wide = jnp.broadcast_to(col, (depth, tokens))
            for m in range(sources):
                target = tgt_refs[group][at, m, pl.ds(l, 1), :]
                row = jnp.sum(jnp.where(here == target, wide, 0.0), axis=0, keepdims=True)
                x_ref[0, pl.ds((me ^ m) * n + g, 1), :] = row

    if mode == "begin":
        take(own_ref, places[0], z, True)
    for h_ref, (i, d) in zip(others, pairs):
        up, behind = heading(z, n, i)
        place = (places[d][0], up * places[d][1] + (1 - up) * places[n - d][1])

        @pl.when(behind >= d)
        def _():
            take(h_ref, place, z + d * (1 - 2 * up), False)


def weights(sc, own, got, sets, places, w, base, mode, held):
    n = len(places)
    distances = range(1, n - 1) if mode == "begin" else [n - 1]
    pairs = [(i, d) for d in distances for i in arrivals(n, d)]
    _, total, depth, part = sets[0][0].shape
    count, _, hidden = got[0][0].shape
    _, sources, _, tokens = sets[0][1].shape
    chunk = pl.BlockSpec((1, depth, hidden), lambda l, sc: (l, 0, 0))
    block = pl.BlockSpec((part, hidden), lambda l, sc: (0, base + l))
    lines = pl.BlockSpec((1, sources * n, tokens), lambda l, sc: (l, 0, 0))
    args, specs = [], []
    if mode == "begin":
        args.append(own)
        specs.append(pl.BlockSpec((1, depth, hidden), lambda l, sc: (base + l, 0, 0)))
    args += [got[i][d - 1] for i, d in pairs]
    specs += [chunk] * len(pairs)
    for rows, _ in sets:
        args.append(rows)
        specs.append(
            pl.BlockSpec((rows.shape[0], 1, depth, part), lambda l, sc: (0, base + l, 0, 0))
        )
    if mode != "end":
        for _, tgt in sets:
            args.append(tgt)
            specs.append(pl.BlockSpec(tgt.shape, lambda l, sc: (0, 0, 0, 0)))
        args.append(w)
        specs.append(block)
    if held is not None:
        args.append(held)
        inner = {"begin": pl.BlockSpec(memory_space=pl.ANY), "parts": lines, "end": block}
        specs.append(inner[mode])
    grads = jax.ShapeDtypeStruct((part, total * hidden), F32)
    rest = jax.ShapeDtypeStruct((count, sources * n, tokens), F32)
    outs = {"begin": ([grads, rest], [block, lines]), "parts": (rest, lines), "end": (grads, block)}
    flops = 2 * (len(pairs) + 1) * count * depth * part * hidden
    return pl.pallas_call(
        functools.partial(weight_kernel, n, places, base, pairs, mode),
        grid_spec=pltpu.PrefetchScalarGridSpec(
            num_scalar_prefetch=1, grid=(count,), in_specs=specs, out_specs=outs[mode][1]
        ),
        out_shape=outs[mode][0],
        input_output_aliases={} if held is None else {len(args): 0},
        cost_estimate=cost(
            flops,
            count * (2 * (len(pairs) + 1) * depth * hidden + 2 * n * depth * part + 6 * part * hidden),
        ),
    )(sc, *args)


def shares(expert_of, routes, gates, n_ep):
    ids = expert_of.reshape(n_ep, 1, -1, 1, 1)
    mine = routes[None, None, None] == ids
    return jnp.where(mine, 1.0 / gates.astype(F32), 0.0)


def local(out_grad, gates, routes, expert_slot, hidden_saved, w_down):
    tokens = out_grad.shape[1]
    chosen = routes.shape[2]
    experts = expert_slot.shape[0]
    n_ep = lax.axis_size("ep")
    n = lax.axis_size("dp")
    local_experts = experts // n_ep
    slots = hidden_saved.shape[3]
    hidden = hidden_saved.shape[4]
    depth = n_ep * slots
    z = lax.axis_index("dp").astype(jnp.int32)
    me = lax.axis_index("ep").astype(jnp.int32)
    ids = jnp.arange(experts, dtype=jnp.int32)
    expert_of = jnp.sum(jnp.where(expert_slot[None, :] == ids[:, None], ids[None, :], 0), axis=1)
    sc = jnp.concatenate([jnp.stack([z, me]), expert_of]).astype(jnp.int32)

    swaps = []
    for start in (1, 0):
        pairs = [(i, i + 1) for i in range(start, n - 1, 2)]
        swaps.append(pairs + [(j, i) for i, j in pairs])
    chunks = CHUNKS if local_experts % CHUNKS == 0 else 1
    count = local_experts // chunks
    saved = hidden_saved.reshape(local_experts, depth, hidden)

    packed = pack(out_grad[0], routes[0].T, gates[0].T, n)
    saved, packed = lax.optimization_barrier((saved, packed))
    first = sorted({1, n - 1})
    orders = [first, [d for d in range(n) if d not in first]]
    arrived = list(packed)
    for order in orders:
        for d in order:
            if d > 0:
                shift = [(j, (j + d) % n) for j in range(n)]
                arrived[d] = lax.ppermute(packed[d], "dp", shift)

    got = [[[], []] for _ in range(chunks)]
    source = saved
    for c in range(chunks):
        if c > 0:
            source, arrived[1] = lax.optimization_barrier((source, arrived[1]))
        part = lax.slice_in_dim(source, c * count, (c + 1) * count, axis=0)
        for i in range(2):
            got[c][i].append(lax.ppermute(part, "dp", swaps[i]))

    places = [None] * n
    sets = []
    for i, order in enumerate(orders):
        for at, d in enumerate(order):
            places[d] = (i, at)
        pieces = [jnp.stack([arrived[d] for d in order])] + [None] * (n_ep - 1)
        for m in range(2, n_ep, 2):
            pieces[m] = lax.ppermute(pieces[0], "ep", [(e, e ^ m) for e in range(n_ep)])
        for m in range(0, n_ep, 2):
            pieces[m + 1] = lax.ppermute(pieces[m], "ep", [(e, e ^ 1) for e in range(n_ep)])
        sets.append(dispatch(sc, pieces, local_experts, slots, tokens, chosen))
    rows = [(sets[i][0], at) for i, at in places]
    own = own_part(rows, w_down)

    weight_grad, parts = None, [None] * chunks
    for t in range(2, n + 1):
        for c in range(chunks):
            base = c * count
            a, b = got[c][0][-1], got[c][1][-1]
            if (t == n - 1 and c > 0) or (t == n and c == 0):
                a, b, weight_grad = lax.optimization_barrier((a, b, weight_grad))
            if t == n and c == chunks - 1:
                for e in range(chunks):
                    parts[e] = weights(
                        sc, saved, got[e], sets, places, w_down, e * count, "parts", parts[e]
                    )
                ready = jnp.concatenate(parts, axis=0).transpose(1, 0, 2)
                a, b, ready, own = lax.optimization_barrier((a, b, ready, own))
                back = lax.all_to_all(ready, ("ep", "dp"), split_axis=0, concat_axis=0, tiled=True)
            a, b = step(sc, a, b, rows, w_down, n, t, base)
            got[c][1].append(lax.ppermute(a, "dp", swaps[1]))
            got[c][0].append(lax.ppermute(b, "dp", swaps[0]))
            if t == n - 1:
                weight_grad, parts[c] = weights(
                    sc, saved, got[c], sets, places, w_down, base, "begin", weight_grad
                )
    for c in range(chunks):
        weight_grad = weights(
            sc, saved, got[c], sets, places, w_down, c * count, "end", weight_grad
        )
    for c in range(chunks):
        base = c * count
        if c < chunks - 1:
            total = lax.slice_in_dim(own, base, base + count, axis=0).astype(F32)
            for part in got[c]:
                total = total + part[-1].astype(F32)
            own = lax.dynamic_update_slice_in_dim(own, total.astype(BF), base, axis=0)
            own, weight_grad, got[-1] = lax.optimization_barrier((own, weight_grad, got[-1]))
    inverse = shares(expert_of, routes[0].T, gates[0].T, n_ep)
    total = own.astype(F32)
    for part in got[-1]:
        wide = ((local_experts - count, 0), (0, 0), (0, 0))
        total = total + jnp.pad(part[-1], wide).astype(F32)
    hidden_grad = total.astype(BF)
    back = back.reshape(n_ep, n, local_experts, 1, tokens)
    gate_grad = jnp.sum(back * inverse, axis=(0, 1, 2)).T[None]
    return (hidden_grad.reshape(hidden_saved.shape), gate_grad, weight_grad)


def solution(mesh):
    return jax.shard_map(
        local,
        mesh=mesh,
        in_specs=(
            P("dp", "ep", None),
            P("dp", "ep", None),
            P("dp", "ep", None),
            P(),
            P("dp", "ep", None, None, None),
            P("dp", "ep"),
        ),
        out_specs=(P("dp", "ep", None, None, None), P("dp", "ep", None), P("dp", "ep")),
        check_vma=False,
    )
```

```python
import functools

import jax
import jax.numpy as jnp
from jax import lax
from jax.experimental import pallas as pl
from jax.experimental.pallas import tpu as pltpu
from jax.sharding import PartitionSpec as P


BF = jnp.bfloat16
F32 = jnp.float32
CHUNKS = 2
ROOM = 32 << 20


def cost(flops, nbytes):
    return pl.CostEstimate(flops=int(flops), bytes_accessed=int(nbytes), transcendentals=0)


def dot(a, b):
    return jnp.dot(a, b, preferred_element_type=F32)


def pack_kernel(n, x_ref, r_ref, g_ref, *outs):
    chosen, tokens = r_ref.shape
    part = outs[0].shape[1]
    z = lax.axis_index("dp")
    for d in range(n):
        k = lax.rem(z + d, n)
        outs[d][:tokens, :] = x_ref[:, pl.ds(pl.multiple_of(k * part, part), part)]
        outs[d][tokens:, :] = jnp.zeros((outs[d].shape[0] - tokens, part), BF)
        outs[d][tokens : tokens + chosen, :tokens] = r_ref[...].astype(F32).astype(BF)
        outs[d][tokens : tokens + chosen, tokens : 2 * tokens] = g_ref[...]


def pack(x, routes, gates, n):
    tokens, width = x.shape
    chosen = routes.shape[0]
    part = width // n
    height = tokens + -(-chosen // 8) * 8
    return pl.pallas_call(
        functools.partial(pack_kernel, n),
        out_shape=[jax.ShapeDtypeStruct((height, part), BF)] * n,
        cost_estimate=cost(0, 4 * tokens * width),
        name="pack",
    )(x, routes, gates)


def dispatch_kernel(dims, sc, *refs):
    sources, local_experts, slots, tokens, chosen = dims
    pieces, (rows_ref, tgt_ref), (hit, gate) = refs[:sources], refs[sources:-2], refs[-2:]
    pad = tgt_ref.shape[2]
    me = sc[1]
    line = lax.broadcasted_iota(jnp.int32, (pad, tokens), 0)
    for m in range(sources):
        named = pieces[m][0, tokens : tokens + chosen, :tokens].astype(F32)
        weights = pieces[m][0, tokens : tokens + chosen, tokens : 2 * tokens].astype(F32)
        hits = jnp.zeros((pad, tokens), F32)
        vals = jnp.zeros((pad, tokens), F32)
        for l in range(local_experts):
            same = named == sc[2 + me * local_experts + l].astype(F32)
            one = jnp.sum(jnp.where(same, 1.0, 0.0), axis=0, keepdims=True)
            val = jnp.sum(jnp.where(same, weights, 0.0), axis=0, keepdims=True)
            hits = jnp.where(line == l, one, hits)
            vals = jnp.where(line == l, val, vals)
        hit[m * pad : (m + 1) * pad] = hits
        gate[m * pad : (m + 1) * pad] = vals
    earlier = lax.broadcasted_iota(jnp.int32, (tokens, tokens), 0) < lax.broadcasted_iota(
        jnp.int32, (tokens, tokens), 1
    )
    rank = dot(hit[...].astype(BF), jnp.where(earlier, 1.0, 0.0).astype(BF))
    for m in range(sources):
        first = ((me ^ m) * slots).astype(F32)
        block = slice(m * pad, (m + 1) * pad)
        tgt_ref[0, m] = jnp.where(hit[block] > 0.5, rank[block] + first, -1.0)
    if slots % 16 == 0:
        place = lax.broadcasted_iota(jnp.int32, (slots, tokens), 0).astype(F32)
        for m in range(sources):
            s = me ^ m
            here = place + (s * slots).astype(F32)
            pick = [
                jnp.where(
                    here == tgt_ref[0, m, l : l + 1, :],
                    gate[m * pad + l : m * pad + l + 1, :],
                    0.0,
                ).astype(BF)
                for l in range(local_experts)
            ]
            got = dot(jnp.concatenate(pick, axis=0), pieces[m][0, :tokens, :]).astype(BF)
            for l in range(local_experts):
                rows_ref[0, l, pl.ds(pl.multiple_of(s * slots, 16), slots), :] = got[
                    l * slots : (l + 1) * slots
                ]
    else:
        here = lax.broadcasted_iota(jnp.int32, (sources * slots, tokens), 0).astype(F32)
        for l in range(local_experts):
            total = jnp.zeros((sources * slots, rows_ref.shape[3]), F32)
            for m in range(sources):
                pick = jnp.where(
                    here == tgt_ref[0, m, l : l + 1, :],
                    gate[m * pad + l : m * pad + l + 1, :],
                    0.0,
                ).astype(BF)
                total += dot(pick, pieces[m][0, :tokens, :])
            rows_ref[0, l] = total.astype(BF)


def dispatch(sc, pieces, local_experts, slots, tokens, chosen):
    sources = len(pieces)
    n, height, part = pieces[0].shape
    pad = -(-local_experts // 8) * 8
    depth = sources * slots
    return pl.pallas_call(
        functools.partial(dispatch_kernel, (sources, local_experts, slots, tokens, chosen)),
        grid_spec=pltpu.PrefetchScalarGridSpec(
            num_scalar_prefetch=1,
            grid=(n,),
            in_specs=[pl.BlockSpec((1, height, part), lambda g, sc: (g, 0, 0))] * sources,
            out_specs=[
                pl.BlockSpec((1, local_experts, depth, part), lambda d, sc: (d, 0, 0, 0)),
                pl.BlockSpec((1, sources, pad, tokens), lambda d, sc: (d, 0, 0, 0)),
            ],
            scratch_shapes=[pltpu.VMEM((sources * pad, tokens), F32)] * 2,
        ),
        out_shape=[
            jax.ShapeDtypeStruct((n, local_experts, depth, part), BF),
            jax.ShapeDtypeStruct((n, sources, pad, tokens), F32),
        ],
        cost_estimate=cost(
            2 * n * sources * local_experts * slots * tokens * part,
            2 * n * part * (sources * height + local_experts * depth),
        ),
        name="dispatch",
    )(sc, *pieces)


def heading(z, n, i):
    odd = lax.rem(z, 2)
    up = 1 - odd if i == 0 else odd
    return up, up * z + (1 - up) * (n - 1 - z)


def step_kernel(n, t, sc, *refs):
    recvs, rows, w_ref, outs = refs[:2], refs[2:4], refs[4], refs[5:]
    for i in range(2):
        adds = heading(sc[0], n, i)[1] < t - 1

        @pl.when(adds)
        def _():
            u = dot(rows[i][0, 0], w_ref[...])
            outs[i][0] = (recvs[i][0].astype(F32) + u).astype(BF)

        @pl.when(jnp.logical_not(adds))
        def _():
            outs[i][0] = recvs[i][0]


def step(sc, a, b, rows, w, n, t, base):
    count, depth, hidden = a.shape
    part = w.shape[0]
    moved = pl.BlockSpec((1, depth, hidden), lambda l, sc: (l, 0, 0))
    source, up_at = rows[t - 1]
    _, down_at = rows[n + 1 - t]

    def block(i):
        def at(l, sc):
            up = heading(sc[0], n, i)[0]
            return up * up_at + (1 - up) * down_at, base + l, 0, 0

        return pl.BlockSpec((1, 1, depth, part), at)

    return pl.pallas_call(
        functools.partial(step_kernel, n, t),
        grid_spec=pltpu.PrefetchScalarGridSpec(
            num_scalar_prefetch=1,
            grid=(count,),
            in_specs=[
                moved,
                moved,
                block(0),
                block(1),
                pl.BlockSpec((part, hidden), lambda l, sc: (0, base + l)),
            ],
            out_specs=[moved, moved],
        ),
        out_shape=[jax.ShapeDtypeStruct(a.shape, BF)] * 2,
        cost_estimate=cost(
            4 * count * depth * part * hidden,
            2 * count * (4 * depth * hidden + 2 * depth * part + part * hidden),
        ),
        compiler_params=pltpu.CompilerParams(vmem_limit_bytes=ROOM),
        name="step",
    )(sc, a, b, source, source, w)


def last_kernel(base, a_ref, b_ref, own_ref, *rest):
    o_ref, a_in, b_in, total, sem = rest[-5:]
    count, depth, _ = own_ref.shape
    cut = 2 if depth % 32 == 0 else 1
    high = depth // cut
    spots = [(l, pl.ds(h * high, high)) for l in range(count) for h in range(cut)]
    inward = []
    for k, spot in enumerate(spots):
        pair = [
            pltpu.make_async_copy(a_ref.at[spot], a_in.at[spot], sem.at[0, k]),
            pltpu.make_async_copy(b_ref.at[spot], b_in.at[spot], sem.at[1, k]),
        ]
        for copy in pair:
            copy.start()
        inward.append(pair)
    outward = []
    for k, spot in enumerate(spots):
        for copy in inward[k]:
            copy.wait()
        value = a_in[spot].astype(F32) + b_in[spot].astype(F32)
        total[spot] = (value + own_ref[spot].astype(F32)).astype(BF)
        l, rows = spot
        copy = pltpu.make_async_copy(total.at[spot], o_ref.at[base + l, rows], sem.at[2, k])
        copy.start()
        outward.append(copy)
    for copy in outward:
        copy.wait()


def last(a, b, own, base, held, total):
    inner = pl.BlockSpec(memory_space=pltpu.VMEM)
    outer = pl.BlockSpec(memory_space=pl.ANY)
    extra = [] if held is None else [held]
    return pl.pallas_call(
        functools.partial(last_kernel, base),
        in_specs=[outer, outer, inner] + [outer] * len(extra),
        out_specs=outer,
        out_shape=jax.ShapeDtypeStruct((total,) + a.shape[1:], BF),
        scratch_shapes=[pltpu.VMEM(a.shape, BF)] * 3
        + [pltpu.SemaphoreType.DMA((3, 2 * a.shape[0]))],
        input_output_aliases={3: 0} if extra else {},
        compiler_params=pltpu.CompilerParams(vmem_limit_bytes=16 * a.size),
        cost_estimate=cost(2 * a.size, 8 * a.size),
        name="last",
    )(a, b, own, *extra)


def own_kernel(rows_ref, w_ref, o_ref):
    o_ref[0] = dot(rows_ref[0, 0], w_ref[...]).astype(BF)


def own_part(rows, w):
    rows, at = rows[0]
    _, total, depth, part = rows.shape
    hidden = w.shape[1] // total
    return pl.pallas_call(
        own_kernel,
        grid=(total,),
        in_specs=[
            pl.BlockSpec((1, 1, depth, part), lambda l: (at, l, 0, 0)),
            pl.BlockSpec((part, hidden), lambda l: (0, l)),
        ],
        out_specs=pl.BlockSpec((1, depth, hidden), lambda l: (l, 0, 0)),
        out_shape=jax.ShapeDtypeStruct((total, depth, hidden), BF),
        cost_estimate=cost(
            2 * total * depth * part * hidden,
            2 * total * (depth * hidden + depth * part + part * hidden),
        ),
        name="own_part",
    )(rows, w)


def arrivals(n, d):
    found = []
    for i in range(2):
        for z in range(n):
            up = 1 - z % 2 if i == 0 else z % 2
            if (z if up else n - 1 - z) >= d and i not in found:
                found.append(i)
    return found


def weight_kernel(n, places, base, pairs, mode, sc, *refs):
    refs = list(refs)
    sets = 1 + max(p for p, _ in places)
    own_ref = refs.pop(0) if mode == "begin" else None
    others = [refs.pop(0) for _ in pairs]
    rows_refs = [refs.pop(0) for _ in range(sets)]
    if mode != "end":
        tgt_refs = [refs.pop(0) for _ in range(sets)]
        w_ref = refs.pop(0)
        x_ref = refs[-1]
        sources, tokens = tgt_refs[0].shape[1], tgt_refs[0].shape[3]
    o_ref = {"begin": refs[-2], "parts": None, "end": refs[-1]}[mode]
    z, me = sc[0], sc[1]
    l = base + pl.program_id(0)
    depth = rows_refs[0].shape[2]
    if mode != "begin":
        refs[-1][...] = refs[0][...]

    def take(h_ref, place, g, fresh):
        group, at = place
        rows = rows_refs[group][at, 0]
        h = h_ref[0]
        if mode != "parts":
            grad = lax.dot_general(rows, h, (((0,), (0,)), ((), ())), preferred_element_type=F32)
            if fresh:
                o_ref[...] = grad
            else:
                o_ref[...] += grad
        if mode != "end":
            here = lax.broadcasted_iota(jnp.int32, (depth, tokens), 0).astype(F32)
            u = dot(rows, w_ref[...])
            col = jnp.sum(u * h.astype(F32), axis=1, keepdims=True)
            wide = jnp.broadcast_to(col, (depth, tokens))
            for m in range(sources):
                target = tgt_refs[group][at, m, pl.ds(l, 1), :]
                row = jnp.sum(jnp.where(here == target, wide, 0.0), axis=0, keepdims=True)
                x_ref[0, pl.ds((me ^ m) * n + g, 1), :] = row

    if mode == "begin":
        take(own_ref, places[0], z, True)
    for h_ref, (i, d) in zip(others, pairs):
        up, behind = heading(z, n, i)
        place = (places[d][0], up * places[d][1] + (1 - up) * places[n - d][1])

        @pl.when(behind >= d)
        def _():
            take(h_ref, place, z + d * (1 - 2 * up), False)


def weights(sc, own, got, sets, places, w, base, mode, held):
    n = len(places)
    distances = range(1, n - 1) if mode == "begin" else [n - 1]
    pairs = [(i, d) for d in distances for i in arrivals(n, d)]
    _, total, depth, part = sets[0][0].shape
    count, _, hidden = got[0][0].shape
    _, sources, _, tokens = sets[0][1].shape
    chunk = pl.BlockSpec((1, depth, hidden), lambda l, sc: (l, 0, 0))
    block = pl.BlockSpec((part, hidden), lambda l, sc: (0, base + l))
    lines = pl.BlockSpec((1, sources * n, tokens), lambda l, sc: (l, 0, 0))
    args, specs = [], []
    if mode == "begin":
        args.append(own)
        specs.append(pl.BlockSpec((1, depth, hidden), lambda l, sc: (base + l, 0, 0)))
    args += [got[i][d - 1] for i, d in pairs]
    specs += [chunk] * len(pairs)
    for rows, _ in sets:
        args.append(rows)
        specs.append(
            pl.BlockSpec((rows.shape[0], 1, depth, part), lambda l, sc: (0, base + l, 0, 0))
        )
    if mode != "end":
        for _, tgt in sets:
            args.append(tgt)
            specs.append(pl.BlockSpec(tgt.shape, lambda l, sc: (0, 0, 0, 0)))
        args.append(w)
        specs.append(block)
    if held is not None:
        args.append(held)
        inner = {"begin": pl.BlockSpec(memory_space=pl.ANY), "parts": lines, "end": block}
        specs.append(inner[mode])
    grads = jax.ShapeDtypeStruct((part, total * hidden), F32)
    rest = jax.ShapeDtypeStruct((count, sources * n, tokens), F32)
    outs = {"begin": ([grads, rest], [block, lines]), "parts": (rest, lines), "end": (grads, block)}
    flops = 2 * (len(pairs) + 1) * count * depth * part * hidden
    return pl.pallas_call(
        functools.partial(weight_kernel, n, places, base, pairs, mode),
        grid_spec=pltpu.PrefetchScalarGridSpec(
            num_scalar_prefetch=1, grid=(count,), in_specs=specs, out_specs=outs[mode][1]
        ),
        out_shape=outs[mode][0],
        input_output_aliases={} if held is None else {len(args): 0},
        cost_estimate=cost(
            flops,
            count * (2 * (len(pairs) + 1) * depth * hidden + 2 * n * depth * part + 6 * part * hidden),
        ),
        compiler_params=pltpu.CompilerParams(vmem_limit_bytes=ROOM),
    )(sc, *args)


def shares(expert_of, routes, gates, n_ep):
    ids = expert_of.reshape(n_ep, 1, -1, 1, 1)
    mine = routes[None, None, None] == ids
    return jnp.where(mine, 1.0 / gates.astype(F32), 0.0)


def local(out_grad, gates, routes, expert_slot, hidden_saved, w_down):
    tokens = out_grad.shape[1]
    chosen = routes.shape[2]
    experts = expert_slot.shape[0]
    n_ep = lax.axis_size("ep")
    n = lax.axis_size("dp")
    local_experts = experts // n_ep
    slots = hidden_saved.shape[3]
    hidden = hidden_saved.shape[4]
    depth = n_ep * slots
    z = lax.axis_index("dp").astype(jnp.int32)
    me = lax.axis_index("ep").astype(jnp.int32)
    ids = jnp.arange(experts, dtype=jnp.int32)
    expert_of = jnp.sum(jnp.where(expert_slot[None, :] == ids[:, None], ids[None, :], 0), axis=1)
    sc = jnp.concatenate([jnp.stack([z, me]), expert_of]).astype(jnp.int32)

    swaps = []
    for start in (1, 0):
        pairs = [(i, i + 1) for i in range(start, n - 1, 2)]
        swaps.append(pairs + [(j, i) for i, j in pairs])
    chunks = CHUNKS if local_experts % CHUNKS == 0 else 1
    count = local_experts // chunks
    saved = hidden_saved.reshape(local_experts, depth, hidden)

    packed = pack(out_grad[0], routes[0].T, gates[0].T, n)
    saved, packed = lax.optimization_barrier((saved, packed))
    first = sorted({1, n - 1})
    orders = [first, [d for d in range(n) if d not in first]]
    arrived = list(packed)
    for order in orders:
        for d in order:
            if d > 0:
                shift = [(j, (j + d) % n) for j in range(n)]
                arrived[d] = lax.ppermute(packed[d], "dp", shift)

    got = [[[], []] for _ in range(chunks)]
    source = saved
    for c in range(chunks):
        if c > 0:
            source, arrived[1] = lax.optimization_barrier((source, arrived[1]))
        part = lax.slice_in_dim(source, c * count, (c + 1) * count, axis=0)
        for i in range(2):
            got[c][i].append(lax.ppermute(part, "dp", swaps[i]))

    places = [None] * n
    sets = []
    for i, order in enumerate(orders):
        for at, d in enumerate(order):
            places[d] = (i, at)
        pieces = [jnp.stack([arrived[d] for d in order])] + [None] * (n_ep - 1)
        for m in range(2, n_ep, 2):
            pieces[m] = lax.ppermute(pieces[0], "ep", [(e, e ^ m) for e in range(n_ep)])
        for m in range(0, n_ep, 2):
            pieces[m + 1] = lax.ppermute(pieces[m], "ep", [(e, e ^ 1) for e in range(n_ep)])
        sets.append(dispatch(sc, pieces, local_experts, slots, tokens, chosen))
    rows = [(sets[i][0], at) for i, at in places]
    own = own_part(rows, w_down)

    weight_grad, parts = None, [None] * chunks
    for t in range(2, n + 1):
        for c in range(chunks):
            base = c * count
            a, b = got[c][0][-1], got[c][1][-1]
            if (t == n - 1 and c > 0) or (t == n and c == 0):
                a, b, weight_grad = lax.optimization_barrier((a, b, weight_grad))
            if t == n and c == chunks - 1:
                for e in range(chunks):
                    parts[e] = weights(
                        sc, saved, got[e], sets, places, w_down, e * count, "parts", parts[e]
                    )
                ready = jnp.concatenate(parts, axis=0).transpose(1, 0, 2)
                a, b, ready, own = lax.optimization_barrier((a, b, ready, own))
                back = lax.all_to_all(ready, ("ep", "dp"), split_axis=0, concat_axis=0, tiled=True)
            a, b = step(sc, a, b, rows, w_down, n, t, base)
            got[c][1].append(lax.ppermute(a, "dp", swaps[1]))
            got[c][0].append(lax.ppermute(b, "dp", swaps[0]))
            if t == n - 1:
                weight_grad, parts[c] = weights(
                    sc, saved, got[c], sets, places, w_down, base, "begin", weight_grad
                )
    for c in range(chunks):
        weight_grad = weights(
            sc, saved, got[c], sets, places, w_down, c * count, "end", weight_grad
        )
    hidden_grad = None
    for c in range(chunks):
        base = c * count
        a, b = got[c][0][-1], got[c][1][-1]
        mine = lax.slice_in_dim(own, base, base + count, axis=0)
        if c == 0:
            mine, weight_grad = lax.optimization_barrier((mine, weight_grad))
        hidden_grad = last(a, b, mine, base, hidden_grad, local_experts)
    inverse = shares(expert_of, routes[0].T, gates[0].T, n_ep)
    back = back.reshape(n_ep, n, local_experts, 1, tokens)
    gate_grad = jnp.sum(back * inverse, axis=(0, 1, 2)).T[None]
    return (hidden_grad.reshape(hidden_saved.shape), gate_grad, weight_grad)


def solution(mesh):
    return jax.shard_map(
        local,
        mesh=mesh,
        in_specs=(
            P("dp", "ep", None),
            P("dp", "ep", None),
            P("dp", "ep", None),
            P(),
            P("dp", "ep", None, None, None),
            P("dp", "ep"),
        ),
        out_specs=(P("dp", "ep", None, None, None), P("dp", "ep", None), P("dp", "ep")),
        check_vma=False,
    )
```

```python
import functools

import jax
import jax.numpy as jnp
from jax import lax
from jax.experimental import pallas as pl
from jax.experimental.pallas import tpu as pltpu
from jax.sharding import PartitionSpec as P


BF = jnp.bfloat16
F32 = jnp.float32
CHUNKS = 2
PIECES = 4
ROOM = 32 << 20


def cost(flops, nbytes):
    return pl.CostEstimate(flops=int(flops), bytes_accessed=int(nbytes), transcendentals=0)


def dot(a, b):
    return jnp.dot(a, b, preferred_element_type=F32)


def pack_kernel(n, x_ref, r_ref, g_ref, *outs):
    chosen, tokens = r_ref.shape
    part = outs[0].shape[1]
    z = lax.axis_index("dp")
    for d in range(n):
        k = lax.rem(z + d, n)
        outs[d][:tokens, :] = x_ref[:, pl.ds(pl.multiple_of(k * part, part), part)]
        outs[d][tokens:, :] = jnp.zeros((outs[d].shape[0] - tokens, part), BF)
        outs[d][tokens : tokens + chosen, :tokens] = r_ref[...].astype(F32).astype(BF)
        outs[d][tokens : tokens + chosen, tokens : 2 * tokens] = g_ref[...]


def pack(x, routes, gates, n):
    tokens, width = x.shape
    chosen = routes.shape[0]
    part = width // n
    height = tokens + -(-chosen // 8) * 8
    return pl.pallas_call(
        functools.partial(pack_kernel, n),
        out_shape=[jax.ShapeDtypeStruct((height, part), BF)] * n,
        cost_estimate=cost(0, 4 * tokens * width),
        name="pack",
    )(x, routes, gates)


def dispatch_kernel(dims, sc, *refs):
    sources, local_experts, slots, tokens, chosen = dims
    pieces, (rows_ref, tgt_ref), (hit, gate) = refs[:sources], refs[sources:-2], refs[-2:]
    pad = tgt_ref.shape[2]
    me = sc[1]
    line = lax.broadcasted_iota(jnp.int32, (pad, tokens), 0)
    for m in range(sources):
        named = pieces[m][0, tokens : tokens + chosen, :tokens].astype(F32)
        weights = pieces[m][0, tokens : tokens + chosen, tokens : 2 * tokens].astype(F32)
        hits = jnp.zeros((pad, tokens), F32)
        vals = jnp.zeros((pad, tokens), F32)
        for l in range(local_experts):
            same = named == sc[2 + me * local_experts + l].astype(F32)
            one = jnp.sum(jnp.where(same, 1.0, 0.0), axis=0, keepdims=True)
            val = jnp.sum(jnp.where(same, weights, 0.0), axis=0, keepdims=True)
            hits = jnp.where(line == l, one, hits)
            vals = jnp.where(line == l, val, vals)
        hit[m * pad : (m + 1) * pad] = hits
        gate[m * pad : (m + 1) * pad] = vals
    earlier = lax.broadcasted_iota(jnp.int32, (tokens, tokens), 0) < lax.broadcasted_iota(
        jnp.int32, (tokens, tokens), 1
    )
    rank = dot(hit[...].astype(BF), jnp.where(earlier, 1.0, 0.0).astype(BF))
    for m in range(sources):
        first = ((me ^ m) * slots).astype(F32)
        block = slice(m * pad, (m + 1) * pad)
        tgt_ref[0, m] = jnp.where(hit[block] > 0.5, rank[block] + first, -1.0)
    if slots % 16 == 0:
        place = lax.broadcasted_iota(jnp.int32, (slots, tokens), 0).astype(F32)
        for m in range(sources):
            s = me ^ m
            here = place + (s * slots).astype(F32)
            pick = [
                jnp.where(
                    here == tgt_ref[0, m, l : l + 1, :],
                    gate[m * pad + l : m * pad + l + 1, :],
                    0.0,
                ).astype(BF)
                for l in range(local_experts)
            ]
            got = dot(jnp.concatenate(pick, axis=0), pieces[m][0, :tokens, :]).astype(BF)
            for l in range(local_experts):
                rows_ref[0, l, pl.ds(pl.multiple_of(s * slots, 16), slots), :] = got[
                    l * slots : (l + 1) * slots
                ]
    else:
        here = lax.broadcasted_iota(jnp.int32, (sources * slots, tokens), 0).astype(F32)
        for l in range(local_experts):
            total = jnp.zeros((sources * slots, rows_ref.shape[3]), F32)
            for m in range(sources):
                pick = jnp.where(
                    here == tgt_ref[0, m, l : l + 1, :],
                    gate[m * pad + l : m * pad + l + 1, :],
                    0.0,
                ).astype(BF)
                total += dot(pick, pieces[m][0, :tokens, :])
            rows_ref[0, l] = total.astype(BF)


def dispatch(sc, pieces, local_experts, slots, tokens, chosen):
    sources = len(pieces)
    n, height, part = pieces[0].shape
    pad = -(-local_experts // 8) * 8
    depth = sources * slots
    return pl.pallas_call(
        functools.partial(dispatch_kernel, (sources, local_experts, slots, tokens, chosen)),
        grid_spec=pltpu.PrefetchScalarGridSpec(
            num_scalar_prefetch=1,
            grid=(n,),
            in_specs=[pl.BlockSpec((1, height, part), lambda g, sc: (g, 0, 0))] * sources,
            out_specs=[
                pl.BlockSpec((1, local_experts, depth, part), lambda d, sc: (d, 0, 0, 0)),
                pl.BlockSpec((1, sources, pad, tokens), lambda d, sc: (d, 0, 0, 0)),
            ],
            scratch_shapes=[pltpu.VMEM((sources * pad, tokens), F32)] * 2,
        ),
        out_shape=[
            jax.ShapeDtypeStruct((n, local_experts, depth, part), BF),
            jax.ShapeDtypeStruct((n, sources, pad, tokens), F32),
        ],
        cost_estimate=cost(
            2 * n * sources * local_experts * slots * tokens * part,
            2 * n * part * (sources * height + local_experts * depth),
        ),
        name="dispatch",
    )(sc, *pieces)


def heading(z, n, i):
    odd = lax.rem(z, 2)
    up = 1 - odd if i == 0 else odd
    return up, up * z + (1 - up) * (n - 1 - z)


def step_kernel(n, t, sc, *refs):
    recvs, rows, w_ref, outs = refs[:2], refs[2:4], refs[4], refs[5:]
    for i in range(2):
        adds = heading(sc[0], n, i)[1] < t - 1

        @pl.when(adds)
        def _():
            u = dot(rows[i][0, 0], w_ref[...])
            outs[i][0] = (recvs[i][0].astype(F32) + u).astype(BF)

        @pl.when(jnp.logical_not(adds))
        def _():
            outs[i][0] = recvs[i][0]


def step(sc, a, b, rows, w, n, t, base):
    count, depth, hidden = a.shape
    part = w.shape[0]
    moved = pl.BlockSpec((1, depth, hidden), lambda l, sc: (l, 0, 0))
    source, up_at = rows[t - 1]
    _, down_at = rows[n + 1 - t]

    def block(i):
        def at(l, sc):
            up = heading(sc[0], n, i)[0]
            return up * up_at + (1 - up) * down_at, base + l, 0, 0

        return pl.BlockSpec((1, 1, depth, part), at)

    return pl.pallas_call(
        functools.partial(step_kernel, n, t),
        grid_spec=pltpu.PrefetchScalarGridSpec(
            num_scalar_prefetch=1,
            grid=(count,),
            in_specs=[
                moved,
                moved,
                block(0),
                block(1),
                pl.BlockSpec((part, hidden), lambda l, sc: (0, base + l)),
            ],
            out_specs=[moved, moved],
        ),
        out_shape=[jax.ShapeDtypeStruct(a.shape, BF)] * 2,
        cost_estimate=cost(
            4 * count * depth * part * hidden,
            2 * count * (4 * depth * hidden + 2 * depth * part + part * hidden),
        ),
        compiler_params=pltpu.CompilerParams(vmem_limit_bytes=ROOM),
        name="step",
    )(sc, a, b, source, source, w)


def last_kernel(base, a_ref, b_ref, own_ref, *rest):
    o_ref, a_in, b_in, total, sem = rest[-5:]
    count, depth, _ = own_ref.shape
    cut = PIECES if depth % (16 * PIECES) == 0 else 1
    high = depth // cut
    spots = [(l, pl.ds(h * high, high)) for l in range(count) for h in range(cut)]
    inward = []
    for k, spot in enumerate(spots):
        pair = [
            pltpu.make_async_copy(a_ref.at[spot], a_in.at[spot], sem.at[0, k]),
            pltpu.make_async_copy(b_ref.at[spot], b_in.at[spot], sem.at[1, k]),
        ]
        for copy in pair:
            copy.start()
        inward.append(pair)
    outward = []
    for k, spot in enumerate(spots):
        for copy in inward[k]:
            copy.wait()
        value = a_in[spot].astype(F32) + b_in[spot].astype(F32)
        total[spot] = (value + own_ref[spot].astype(F32)).astype(BF)
        l, rows = spot
        copy = pltpu.make_async_copy(total.at[spot], o_ref.at[base + l, rows], sem.at[2, k])
        copy.start()
        outward.append(copy)
    for copy in outward:
        copy.wait()


def last(a, b, own, base, held, total):
    inner = pl.BlockSpec(memory_space=pltpu.VMEM)
    outer = pl.BlockSpec(memory_space=pl.ANY)
    extra = [] if held is None else [held]
    return pl.pallas_call(
        functools.partial(last_kernel, base),
        in_specs=[outer, outer, inner] + [outer] * len(extra),
        out_specs=outer,
        out_shape=jax.ShapeDtypeStruct((total,) + a.shape[1:], BF),
        scratch_shapes=[pltpu.VMEM(a.shape, BF)] * 3
        + [pltpu.SemaphoreType.DMA((3, PIECES * a.shape[0]))],
        input_output_aliases={3: 0} if extra else {},
        compiler_params=pltpu.CompilerParams(vmem_limit_bytes=16 * a.size),
        cost_estimate=cost(2 * a.size, 8 * a.size),
        name="last",
    )(a, b, own, *extra)


def own_kernel(rows_ref, w_ref, o_ref):
    o_ref[0] = dot(rows_ref[0, 0], w_ref[...]).astype(BF)


def own_part(rows, w):
    rows, at = rows[0]
    _, total, depth, part = rows.shape
    hidden = w.shape[1] // total
    return pl.pallas_call(
        own_kernel,
        grid=(total,),
        in_specs=[
            pl.BlockSpec((1, 1, depth, part), lambda l: (at, l, 0, 0)),
            pl.BlockSpec((part, hidden), lambda l: (0, l)),
        ],
        out_specs=pl.BlockSpec((1, depth, hidden), lambda l: (l, 0, 0)),
        out_shape=jax.ShapeDtypeStruct((total, depth, hidden), BF),
        cost_estimate=cost(
            2 * total * depth * part * hidden,
            2 * total * (depth * hidden + depth * part + part * hidden),
        ),
        name="own_part",
    )(rows, w)


def arrivals(n, d):
    found = []
    for i in range(2):
        for z in range(n):
            up = 1 - z % 2 if i == 0 else z % 2
            if (z if up else n - 1 - z) >= d and i not in found:
                found.append(i)
    return found


def weight_kernel(n, places, base, pairs, mode, sc, *refs):
    refs = list(refs)
    sets = 1 + max(p for p, _ in places)
    own_ref = refs.pop(0) if mode == "begin" else None
    others = [refs.pop(0) for _ in pairs]
    rows_refs = [refs.pop(0) for _ in range(sets)]
    if mode != "end":
        tgt_refs = [refs.pop(0) for _ in range(sets)]
        w_ref = refs.pop(0)
        x_ref = refs[-1]
        sources, tokens = tgt_refs[0].shape[1], tgt_refs[0].shape[3]
    o_ref = {"begin": refs[-2], "parts": None, "end": refs[-1]}[mode]
    z, me = sc[0], sc[1]
    l = base + pl.program_id(0)
    depth = rows_refs[0].shape[2]
    if mode != "begin":
        refs[-1][...] = refs[0][...]

    def take(h_ref, place, g, fresh):
        group, at = place
        rows = rows_refs[group][at, 0]
        h = h_ref[0]
        if mode != "parts":
            grad = lax.dot_general(rows, h, (((0,), (0,)), ((), ())), preferred_element_type=F32)
            if fresh:
                o_ref[...] = grad
            else:
                o_ref[...] += grad
        if mode != "end":
            here = lax.broadcasted_iota(jnp.int32, (depth, tokens), 0).astype(F32)
            u = dot(rows, w_ref[...])
            col = jnp.sum(u * h.astype(F32), axis=1, keepdims=True)
            wide = jnp.broadcast_to(col, (depth, tokens))
            for m in range(sources):
                target = tgt_refs[group][at, m, pl.ds(l, 1), :]
                row = jnp.sum(jnp.where(here == target, wide, 0.0), axis=0, keepdims=True)
                x_ref[0, pl.ds((me ^ m) * n + g, 1), :] = row

    if mode == "begin":
        take(own_ref, places[0], z, True)
    for h_ref, (i, d) in zip(others, pairs):
        up, behind = heading(z, n, i)
        place = (places[d][0], up * places[d][1] + (1 - up) * places[n - d][1])

        @pl.when(behind >= d)
        def _():
            take(h_ref, place, z + d * (1 - 2 * up), False)


def weights(sc, own, got, sets, places, w, base, mode, held):
    n = len(places)
    distances = range(1, n - 1) if mode == "begin" else [n - 1]
    pairs = [(i, d) for d in distances for i in arrivals(n, d)]
    _, total, depth, part = sets[0][0].shape
    count, _, hidden = got[0][0].shape
    _, sources, _, tokens = sets[0][1].shape
    chunk = pl.BlockSpec((1, depth, hidden), lambda l, sc: (l, 0, 0))
    block = pl.BlockSpec((part, hidden), lambda l, sc: (0, base + l))
    lines = pl.BlockSpec((1, sources * n, tokens), lambda l, sc: (l, 0, 0))
    args, specs = [], []
    if mode == "begin":
        args.append(own)
        specs.append(pl.BlockSpec((1, depth, hidden), lambda l, sc: (base + l, 0, 0)))
    args += [got[i][d - 1] for i, d in pairs]
    specs += [chunk] * len(pairs)
    for rows, _ in sets:
        args.append(rows)
        specs.append(
            pl.BlockSpec((rows.shape[0], 1, depth, part), lambda l, sc: (0, base + l, 0, 0))
        )
    if mode != "end":
        for _, tgt in sets:
            args.append(tgt)
            specs.append(pl.BlockSpec(tgt.shape, lambda l, sc: (0, 0, 0, 0)))
        args.append(w)
        specs.append(block)
    if held is not None:
        args.append(held)
        inner = {"begin": pl.BlockSpec(memory_space=pl.ANY), "parts": lines, "end": block}
        specs.append(inner[mode])
    grads = jax.ShapeDtypeStruct((part, total * hidden), F32)
    rest = jax.ShapeDtypeStruct((count, sources * n, tokens), F32)
    outs = {"begin": ([grads, rest], [block, lines]), "parts": (rest, lines), "end": (grads, block)}
    flops = 2 * (len(pairs) + 1) * count * depth * part * hidden
    return pl.pallas_call(
        functools.partial(weight_kernel, n, places, base, pairs, mode),
        grid_spec=pltpu.PrefetchScalarGridSpec(
            num_scalar_prefetch=1, grid=(count,), in_specs=specs, out_specs=outs[mode][1]
        ),
        out_shape=outs[mode][0],
        input_output_aliases={} if held is None else {len(args): 0},
        cost_estimate=cost(
            flops,
            count * (2 * (len(pairs) + 1) * depth * hidden + 2 * n * depth * part + 6 * part * hidden),
        ),
        compiler_params=pltpu.CompilerParams(vmem_limit_bytes=ROOM),
    )(sc, *args)


def shares(expert_of, routes, gates, n_ep):
    ids = expert_of.reshape(n_ep, 1, -1, 1, 1)
    mine = routes[None, None, None] == ids
    return jnp.where(mine, 1.0 / gates.astype(F32), 0.0)


def local(out_grad, gates, routes, expert_slot, hidden_saved, w_down):
    tokens = out_grad.shape[1]
    chosen = routes.shape[2]
    experts = expert_slot.shape[0]
    n_ep = lax.axis_size("ep")
    n = lax.axis_size("dp")
    local_experts = experts // n_ep
    slots = hidden_saved.shape[3]
    hidden = hidden_saved.shape[4]
    depth = n_ep * slots
    z = lax.axis_index("dp").astype(jnp.int32)
    me = lax.axis_index("ep").astype(jnp.int32)
    ids = jnp.arange(experts, dtype=jnp.int32)
    expert_of = jnp.sum(jnp.where(expert_slot[None, :] == ids[:, None], ids[None, :], 0), axis=1)
    sc = jnp.concatenate([jnp.stack([z, me]), expert_of]).astype(jnp.int32)

    swaps = []
    for start in (1, 0):
        pairs = [(i, i + 1) for i in range(start, n - 1, 2)]
        swaps.append(pairs + [(j, i) for i, j in pairs])
    chunks = CHUNKS if local_experts % CHUNKS == 0 else 1
    count = local_experts // chunks
    saved = hidden_saved.reshape(local_experts, depth, hidden)

    packed = pack(out_grad[0], routes[0].T, gates[0].T, n)
    saved, packed = lax.optimization_barrier((saved, packed))
    first = sorted({1, n - 1})
    orders = [first, [d for d in range(n) if d not in first]]
    arrived = list(packed)
    for order in orders:
        for d in order:
            if d > 0:
                shift = [(j, (j + d) % n) for j in range(n)]
                arrived[d] = lax.ppermute(packed[d], "dp", shift)

    got = [[[], []] for _ in range(chunks)]
    source = saved
    for c in range(chunks):
        if c > 0:
            source, arrived[1] = lax.optimization_barrier((source, arrived[1]))
        part = lax.slice_in_dim(source, c * count, (c + 1) * count, axis=0)
        for i in range(2):
            got[c][i].append(lax.ppermute(part, "dp", swaps[i]))

    places = [None] * n
    sets = []
    for i, order in enumerate(orders):
        for at, d in enumerate(order):
            places[d] = (i, at)
        pieces = [jnp.stack([arrived[d] for d in order])] + [None] * (n_ep - 1)
        for m in range(2, n_ep, 2):
            pieces[m] = lax.ppermute(pieces[0], "ep", [(e, e ^ m) for e in range(n_ep)])
        for m in range(0, n_ep, 2):
            pieces[m + 1] = lax.ppermute(pieces[m], "ep", [(e, e ^ 1) for e in range(n_ep)])
        sets.append(dispatch(sc, pieces, local_experts, slots, tokens, chosen))
    rows = [(sets[i][0], at) for i, at in places]
    own = own_part(rows, w_down)

    weight_grad, parts = None, [None] * chunks
    for t in range(2, n + 1):
        for c in range(chunks):
            base = c * count
            a, b = got[c][0][-1], got[c][1][-1]
            if (t == n - 1 and c > 0) or (t == n and c == 0):
                a, b, weight_grad = lax.optimization_barrier((a, b, weight_grad))
            if t == n and c == chunks - 1:
                for e in range(chunks):
                    parts[e] = weights(
                        sc, saved, got[e], sets, places, w_down, e * count, "parts", parts[e]
                    )
                ready = jnp.concatenate(parts, axis=0).transpose(1, 0, 2)
                a, b, ready, own = lax.optimization_barrier((a, b, ready, own))
                back = lax.all_to_all(ready, ("ep", "dp"), split_axis=0, concat_axis=0, tiled=True)
            a, b = step(sc, a, b, rows, w_down, n, t, base)
            got[c][1].append(lax.ppermute(a, "dp", swaps[1]))
            got[c][0].append(lax.ppermute(b, "dp", swaps[0]))
            if t == n - 1:
                weight_grad, parts[c] = weights(
                    sc, saved, got[c], sets, places, w_down, base, "begin", weight_grad
                )
    for c in range(chunks):
        weight_grad = weights(
            sc, saved, got[c], sets, places, w_down, c * count, "end", weight_grad
        )
    hidden_grad = None
    for c in range(chunks):
        base = c * count
        a, b = got[c][0][-1], got[c][1][-1]
        mine = lax.slice_in_dim(own, base, base + count, axis=0)
        if c == 0:
            mine, weight_grad = lax.optimization_barrier((mine, weight_grad))
        hidden_grad = last(a, b, mine, base, hidden_grad, local_experts)
    inverse = shares(expert_of, routes[0].T, gates[0].T, n_ep)
    back = back.reshape(n_ep, n, local_experts, 1, tokens)
    gate_grad = jnp.sum(back * inverse, axis=(0, 1, 2)).T[None]
    return (hidden_grad.reshape(hidden_saved.shape), gate_grad, weight_grad)


def solution(mesh):
    return jax.shard_map(
        local,
        mesh=mesh,
        in_specs=(
            P("dp", "ep", None),
            P("dp", "ep", None),
            P("dp", "ep", None),
            P(),
            P("dp", "ep", None, None, None),
            P("dp", "ep"),
        ),
        out_specs=(P("dp", "ep", None, None, None), P("dp", "ep", None), P("dp", "ep")),
        check_vma=False,
    )
```
